256 devices in a mesh: ctx: 128 (over z, y_hi, x, core), head: 2 (over y_lo).
Axes of the slice: x: 4, y: 4 (y_hi: 2, y_lo: 2; y = y_hi * 2 + y_lo), z: 8, core: 2. Of those that a mesh axis runs over, the one named last changes fastest.
Arguments:
- queries: bfloat16 [2, 16384, 2048], P(None, 'ctx', 'head'), may hold values from -8 to 8
- keys_values: bfloat16 [2, 2, 16384, 512], P(None, None, 'ctx', 'head'), may hold values from -12 to 12
- grad_layer: bfloat16 [2, 16384, 4096], P(None, 'ctx'), may hold values from -0.29882812 to 0.29882812
- out_proj: bfloat16 [4096, 2048], P('ctx', 'head'), may hold values from -0.125 to 0.125
- doc_layout: int32 [3, 16384], P(None, 'ctx'), may hold values from 0 to 16384, as said below
Outputs:
- layer_out: bfloat16 [2, 16384, 4096], P(None, 'ctx', 'head')
- grad_queries: float32 [2, 16384, 2048], P(None, 'ctx', 'head')
- grad_keys_values: float32 [2, 2, 16384, 512], P(None, None, 'ctx', 'head')
The draws below stay inside these ranges and needn't reach their ends.
Inputs may be any that keep to these rules, and one draw needn't show every extreme that they name: doc_layout[0, p] and doc_layout[1, p] are the first position and one past the last position of the document that holds position p; documents are consecutive runs covering all 16384 positions, each starting at a multiple of 32 and holding a multiple of 32 positions, at most 896, one of exactly 896; doc_layout[2, p] is that document's diffusion block size, a power of two from 4 to 32, and the document of 896 positions has 32.
All inputs are finite; a program needn't handle non-finite values.
Results may differ from the reference program's by a relative error of at most 0.009.
Values may be sent and summed in bfloat16 or wider, within the bound.
A program may use at most 64 MiB of HBM per device.

```python
import math
import jax
import jax.numpy as jnp
from jax import lax

D = 4096
HD = 128
GQ = 4
BMAX = 32
KV_GROUPS = 4
TOKENS = 16384
MAXDOC = 896


def layout_parts(base_key):
    key_len, key_pick, key_block = jax.random.split(jax.random.fold_in(base_key, 11), 3)
    doc_count = TOKENS // BMAX + 1
    lengths = BMAX * jax.random.randint(key_len, (doc_count,), 1, MAXDOC // BMAX + 1)
    picked = jax.random.randint(key_pick, (), 0, max(1, min(4, TOKENS // MAXDOC)))
    doc_slots = jnp.arange(doc_count, dtype=jnp.int32)
    lengths = jnp.where(doc_slots == picked, MAXDOC, lengths).astype(jnp.int32)
    powers = jax.random.randint(key_block, (doc_count,), 2, BMAX.bit_length())
    blocks = jnp.where(doc_slots == picked, BMAX, jnp.left_shift(jnp.ones_like(powers), powers)).astype(jnp.int32)
    doc_ends = jnp.cumsum(lengths).astype(jnp.int32)
    starts = doc_ends - lengths
    return (starts, doc_ends, blocks)


def draw_doc_layout(key, part):
    starts, doc_ends, blocks = layout_parts(key)
    positions = jnp.arange(TOKENS, dtype=jnp.int32)
    which_doc = jnp.searchsorted(doc_ends, positions, side='right').astype(jnp.int32)
    return jnp.stack([starts[which_doc], jnp.minimum(doc_ends[which_doc], TOKENS), blocks[which_doc]]).astype(jnp.int32)


def draw_queries(key, part):
    key_main, key_scale = jax.random.split(jax.random.fold_in(key, 31))
    draw_shape = (2, TOKENS, KV_GROUPS * GQ, HD)
    values = jax.random.normal(key_main, draw_shape, jnp.float32)
    spread = jnp.exp(jax.random.uniform(key_scale, (2, TOKENS, KV_GROUPS * GQ, 1), jnp.float32, math.log(0.5), math.log(2.0)))
    values = jnp.clip(values * spread, -8.0, 8.0)
    return values.reshape(2, TOKENS, KV_GROUPS * GQ * HD).astype(jnp.bfloat16)


def draw_keys_values(key, part):
    key_main, key_scale = jax.random.split(jax.random.fold_in(key, 41))
    draw_shape = (2, 2, TOKENS, KV_GROUPS, HD)
    values = jax.random.normal(key_main, draw_shape, jnp.float32)
    spread = jnp.exp(jax.random.uniform(key_scale, (2, 2, TOKENS, KV_GROUPS, 1), jnp.float32, math.log(0.3), math.log(3.0)))
    values = jnp.clip(values * spread, -12.0, 12.0)
    return values.reshape(2, 2, TOKENS, KV_GROUPS * HD).astype(jnp.bfloat16)


def steps_of(rng, shape, cuts, least, largest):
    level = 1.0
    for axis_at, blocks in cuts:
        steps = jax.random.uniform(jax.random.fold_in(jax.random.fold_in(rng, 6), axis_at), (blocks,), jnp.float32, least / len(cuts), largest / len(cuts))
        level = level * jnp.repeat(jnp.exp(steps), shape[axis_at] // blocks).reshape((-1,) + (1,) * (len(shape) - 1 - axis_at))
    return level


def normal_values(key, extent, width, reach, pieces=(), kind=jnp.bfloat16):
    level = steps_of(key, extent, pieces, -0.22, 0.18) if pieces else 1.0
    result = jax.random.normal(key, extent, jnp.float32) * width * level
    return jnp.minimum(jnp.maximum(result, -reach), reach).astype(kind)


def setup_inputs(seed: int = 0) -> dict:
    key_of = jax.random.split(jax.random.key(seed), 6)
    return {
        "queries": draw_queries(jax.random.fold_in(key_of[5], 71), 0),
        "keys_values": draw_keys_values(jax.random.fold_in(key_of[5], 71), 0),
        "grad_layer": normal_values(key_of[2], (2, TOKENS, D), 0.05, 0.29882812, ((1, 128),)),
        "out_proj": normal_values(key_of[3], (D, KV_GROUPS * GQ * HD), (KV_GROUPS * GQ * HD) ** -0.5, 0.125, ((0, 128), (1, 2))),
        "doc_layout": draw_doc_layout(jax.random.fold_in(key_of[5], 71), 0),
    }


NEGATIVE = -1e30


def visibility(query_copy, key_copy, query_pos, layout, key_pos):
    starts = layout[0][:, None]
    doc_ends = layout[1][:, None]
    block_len = layout[2][:, None]
    key_row = key_pos[None, :]
    inside = (key_row >= starts) & (key_row < doc_ends)
    query_block = (query_pos[:, None] - starts) // block_len
    key_block = (key_row - starts) // block_len
    if query_copy == 0 and key_copy == 0:
        related = key_block == query_block
    elif query_copy == 0:
        related = key_block < query_block
    else:
        related = key_block <= query_block
    return inside & related


def rounded(values):
    return lax.optimization_barrier(values.astype(jnp.bfloat16)).astype(jnp.float32)


def masked_scores(query_rows, key_rows, visible, scale_factor):
    raw = jnp.einsum('tghd,ngd->ghtn', query_rows, key_rows) * scale_factor
    return jnp.where(visible, raw, NEGATIVE)


def masked_exp(scores, visible, shift_by):
    return jnp.where(visible, jnp.exp(scores - shift_by[..., None]), 0.0)


def reference(queries, keys_values, grad_layer, out_proj, doc_layout):
    groups = KV_GROUPS
    scale_factor = HD ** -0.5
    block_rows = 256
    window_len = MAXDOC + block_rows
    query_all = queries.reshape(2, TOKENS, groups, GQ, HD)
    grad_att = jnp.dot(grad_layer.reshape(2 * TOKENS, D), out_proj, preferred_element_type=jnp.float32).astype(jnp.bfloat16)
    grad_all = grad_att.reshape(2, TOKENS, groups, GQ, HD)
    pairs = keys_values.reshape(2, 2, TOKENS, groups, HD)
    noisy_all = pairs[:, 0]
    clean_pad = jnp.pad(pairs[:, 1], ((0, 0), (MAXDOC, 0), (0, 0), (0, 0)))

    def attend(buffers, first_row):
        noisy_grad, clean_grad = buffers
        query_pos = first_row + jnp.arange(block_rows, dtype=jnp.int32)
        wide_pos = first_row - MAXDOC + jnp.arange(window_len, dtype=jnp.int32)
        layout = lax.dynamic_slice_in_dim(doc_layout, first_row, block_rows, 1)
        query_rows = lax.dynamic_slice_in_dim(query_all, first_row, block_rows, 1).astype(jnp.float32)
        grad_rows = lax.dynamic_slice_in_dim(grad_all, first_row, block_rows, 1).astype(jnp.float32)
        near = lax.dynamic_slice_in_dim(noisy_all, first_row, block_rows, 1).astype(jnp.float32)
        wide = lax.dynamic_slice_in_dim(clean_pad, first_row, window_len, 1).astype(jnp.float32)
        seen_noisy = visibility(0, 0, query_pos, layout, query_pos)
        seen_cross = visibility(0, 1, query_pos, layout, wide_pos)
        seen_clean = visibility(1, 1, query_pos, layout, wide_pos)
        score_noisy = masked_scores(query_rows[0], near[0], seen_noisy, scale_factor)
        score_cross = masked_scores(query_rows[0], wide[0], seen_cross, scale_factor)
        score_clean = masked_scores(query_rows[1], wide[0], seen_clean, scale_factor)
        peak_noisy = jnp.maximum(score_noisy.max(-1), score_cross.max(-1))
        log_noisy = peak_noisy + jnp.log(jnp.sum(masked_exp(score_noisy, seen_noisy, peak_noisy), -1)
                                         + jnp.sum(masked_exp(score_cross, seen_cross, peak_noisy), -1))
        peak_clean = score_clean.max(-1)
        log_clean = peak_clean + jnp.log(jnp.sum(masked_exp(score_clean, seen_clean, peak_clean), -1))
        prob_noisy = masked_exp(score_noisy, seen_noisy, log_noisy)
        prob_cross = masked_exp(score_cross, seen_cross, log_noisy)
        prob_clean = masked_exp(score_clean, seen_clean, log_clean)
        half_noisy = rounded(prob_noisy)
        half_cross = rounded(prob_cross)
        half_clean = rounded(prob_clean)
        out_noisy = jnp.einsum('ghtn,ngd->tghd', half_noisy, near[1]) + jnp.einsum('ghtn,ngd->tghd', half_cross, wide[1])
        out_clean = jnp.einsum('ghtn,ngd->tghd', half_clean, wide[1])
        attended = jnp.stack([out_noisy, out_clean]).astype(jnp.bfloat16)
        row_delta = jnp.transpose(jnp.sum(grad_rows * lax.optimization_barrier(attended).astype(jnp.float32), -1), (0, 2, 3, 1))
        flow_noisy = jnp.einsum('tghd,ngd->ghtn', grad_rows[0], near[1])
        flow_cross = jnp.einsum('tghd,ngd->ghtn', grad_rows[0], wide[1])
        flow_clean = jnp.einsum('tghd,ngd->ghtn', grad_rows[1], wide[1])
        dscore_noisy = rounded(prob_noisy * (flow_noisy - row_delta[0][..., None]))
        dscore_cross = rounded(prob_cross * (flow_cross - row_delta[0][..., None]))
        dscore_clean = rounded(prob_clean * (flow_clean - row_delta[1][..., None]))
        dq_noisy = scale_factor * (jnp.einsum('ghtn,ngd->tghd', dscore_noisy, near[0])
                                   + jnp.einsum('ghtn,ngd->tghd', dscore_cross, wide[0]))
        dq_clean = scale_factor * jnp.einsum('ghtn,ngd->tghd', dscore_clean, wide[0])
        noisy_part = jnp.stack([scale_factor * jnp.einsum('ghtn,tghd->ngd', dscore_noisy, query_rows[0]),
                                jnp.einsum('ghtn,tghd->ngd', half_noisy, grad_rows[0])])
        clean_part = jnp.stack([scale_factor * (jnp.einsum('ghtn,tghd->ngd', dscore_cross, query_rows[0])
                                                + jnp.einsum('ghtn,tghd->ngd', dscore_clean, query_rows[1])),
                                jnp.einsum('ghtn,tghd->ngd', half_cross, grad_rows[0])
                                + jnp.einsum('ghtn,tghd->ngd', half_clean, grad_rows[1])])
        noisy_grad = lax.dynamic_update_slice_in_dim(noisy_grad, noisy_part, first_row, 1)
        previous = lax.dynamic_slice_in_dim(clean_grad, first_row, window_len, 1)
        clean_grad = lax.dynamic_update_slice_in_dim(clean_grad, previous + clean_part, first_row, 1)
        return (noisy_grad, clean_grad), (attended, jnp.stack([dq_noisy, dq_clean]))

    starts_all = jnp.arange(TOKENS // block_rows, dtype=jnp.int32) * block_rows
    initial = (jnp.zeros((2, TOKENS, groups, HD), jnp.float32),
               jnp.zeros((2, MAXDOC + TOKENS, groups, HD), jnp.float32))
    (noisy_grad, clean_grad), (att_blocks, dq_blocks) = lax.scan(attend, initial, starts_all)
    att_all = jnp.transpose(att_blocks, (1, 0, 2, 3, 4, 5)).reshape(2 * TOKENS, groups * GQ * HD)
    layer_out = jnp.dot(att_all, out_proj.T, preferred_element_type=jnp.float32).astype(jnp.bfloat16).reshape(2, TOKENS, D)
    grad_queries = jnp.transpose(dq_blocks, (1, 0, 2, 3, 4, 5)).reshape(2, TOKENS, groups * GQ * HD)
    grad_keys_values = jnp.stack([noisy_grad, clean_grad[:, MAXDOC:]], 1).reshape(2, 2, TOKENS, groups * HD)
    return (layer_out, grad_queries, grad_keys_values)
```

```python
import functools
import math

import jax
import jax.numpy as jnp
from jax import lax
from jax.experimental import pallas as pl
from jax.experimental.pallas import tpu as pltpu
from jax.sharding import PartitionSpec as P

F32 = jnp.float32
BF16 = jnp.bfloat16
MESH = pl.DeviceIdType.MESH
NEG = -1e30
SCALE = 128 ** -0.5
EXP2 = SCALE * math.log2(math.e)

NZ, NY, NX = 8, 2, 4
SUBS = (0, 3, 1, 2)
PLANES = (0, 7, 1, 6, 2, 5, 3, 4)


def nt(a, b):
    return lax.dot_general(a, b, (((1,), (1,)), ((), ())), preferred_element_type=F32)


def nn(a, b):
    return lax.dot_general(a, b, (((1,), (0,)), ((), ())), preferred_element_type=F32)


def kernel(
    q_hbm, kv_hbm, g_hbm, w_hbm, lay_hbm,
    out_hbm, dq_hbm, dkv_hbm,
    wbuf, qs, kvw, kvn, gbuf, lay, bias, bnoisy, st, pt, dst, vt, kt,
    att, gacc, lrow, lcol, gs, dl, ypart, ysend, yrecv, yout,
    stage, evens, col, comb, ret, own, dqv, dkvv,
    dsem, ks, kr, ws, wr, pps, ppr, es, er, rs, rr,
):
    ctx = lax.axis_index("ctx")
    hd = lax.axis_index("head")
    core = lax.rem(ctx, 2)
    x = lax.rem(lax.div(ctx, 2), NX)
    yh = lax.rem(lax.div(ctx, 8), NY)
    z = lax.div(ctx, 16)

    def place(z_, y_, x_):
        return ((z_ * NY + y_) * NX + x_) * 2 + core

    xs = [lax.rem(x + d, NX) for d in range(NX)]
    zs = [lax.rem(z + d, NZ) for d in range(NZ)]
    dev_y = (place(z, 1 - yh, x), hd)
    dev_x = [(place(z, yh, xs[1]), hd), (place(z, yh, xs[3]), hd)]
    dev_z = [(place(zs[1], yh, x), hd), (place(zs[7], yh, x), hd)]
    dev_pair = (ctx + 1 - 2 * core, hd)
    dev_head = (ctx, 1 - hd)
    later = [(lax.rem(ctx + 2 * k, 128), hd) for k in range(4)]
    earlier = [(lax.rem(ctx + 128 - 2 * k, 128), hd) for k in range(4)]
    dev_seven = (lax.rem(ctx + 121 + 14 * core, 128), hd)

    def remote(src, dst_ref, send, recv, device):
        return pltpu.make_async_remote_copy(
            src_ref=src, dst_ref=dst_ref, send_sem=send, recv_sem=recv,
            device_id=device, device_id_type=MESH,
        )

    def fetch(src, dst_ref, sem):
        copy = pltpu.make_async_copy(src, dst_ref, sem)
        copy.start()
        return copy

    get_w = fetch(w_hbm, wbuf.at[z, yh, x, core], dsem.at[0])
    get_kv = fetch(kv_hbm.at[:, 1], kvw.at[0], dsem.at[1])
    get_kn = fetch(kv_hbm.at[:, 0], kvn, dsem.at[2])
    get_lay = fetch(lay_hbm, lay, dsem.at[3])
    for copy_id in range(2):
        for head in range(8):
            pb = (head // 4) * 4 + copy_id * 2 + (head % 4) // 2
            fetch(
                q_hbm.at[copy_id, :, pl.ds(head * 128, 128)],
                qs.at[pb, pl.ds((head % 2) * 128, 128)],
                dsem.at[4],
            )
    get_g = fetch(g_hbm, gbuf, dsem.at[5])

    barrier = pltpu.get_barrier_semaphore()
    meet = [dev_y, *dev_x, *dev_z, dev_pair, dev_head, *later[1:], *earlier[1:], dev_seven]
    for device in meet:
        pl.semaphore_signal(barrier, inc=1, device_id=device, device_id_type=MESH)
    pl.semaphore_wait(barrier, len(meet))

    own_kv = kv_hbm.at[:, 1]
    kv_far = [remote(own_kv, kvw.at[2 * k], ks.at[k], kr.at[2 * k], later[k]) for k in (1, 2, 3)]
    kv_seven = remote(own_kv, kvw.at[7], ks.at[0], kr.at[7], dev_seven)
    kv_own = remote(own_kv, kvw.at[1], ks.at[0], kr.at[1], dev_pair)

    w_first = remote(w_hbm, wbuf.at[z, yh, x, core], ws.at[0], wr.at[0], dev_y)
    w_first.start()

    @pl.when(core == 0)
    def _():
        kv_own.start()

    for copy in kv_far:
        copy.start()

    @pl.when(core == 1)
    def _():
        kv_seven.start()

    def kv_pass(k):
        kv_far[k - 1].wait_recv()

        @pl.when(core == 0)
        def _():
            remote(
                kvw.at[2 * k], kvw.at[2 * k + 1], ks.at[3 + k], kr.at[2 * k + 1], dev_pair
            ).start()

        @pl.when(core == 1)
        def _():
            remote(
                kvw.at[2 * k], kvw.at[2 * k - 1], ks.at[3 + k], kr.at[2 * k - 1], dev_pair
            ).start()

    def kv_odd(slot):
        remote(kvw.at[slot], kvw.at[slot], ks.at[0], kr.at[slot], dev_pair).wait_recv()

    sent = ([], [])

    def send_w(core_id, view, device, recv):
        n = len(sent[core_id]) + 1
        src = view()
        remote(src, src, ws.at[n], wr.at[recv], device).start()
        sent[core_id].append(view)

    def wait_w(src, recv):
        remote(src, src, ws.at[0], wr.at[recv], dev_y).wait_recv()

    def passed(core_id, n):
        src = wbuf.at[zs[PLANES[n]], :, :, core_id]
        return remote(src, src, pps.at[n], ppr.at[n], dev_pair)

    def pass_plane(core_id, n):
        passed(core_id, n).start()

    def sub0(dz, dx):
        return wbuf.at[zs[dz], :, xs[dx], 0]

    def zrecv0(way, hop, s):
        return 5 + (way * 4 + hop - 1) * 4 + s

    def ticks0():
        def first():
            get_w.wait()
            w_first.wait_recv()
            for way in range(2):
                send_w(0, lambda: sub0(0, 0), dev_x[way], 1 + way)
            for way in range(2):
                send_w(0, lambda: sub0(0, 0), dev_z[way], zrecv0(way, 1, 0))

        def second():
            for way, (dx, half) in enumerate(((3, 0), (1, 1))):
                wait_w(sub0(0, dx), 1 + way)
                send_w(0, lambda dx=dx, half=half: wbuf.at[z, half, xs[dx], 0], dev_x[way], 3 + way)
                for zway in range(2):
                    send_w(0, lambda dx=dx: sub0(0, dx), dev_z[zway], zrecv0(zway, 1, 1 + way))

        def third():
            for way in range(2):
                wait_w(wbuf.at[z, way, xs[2], 0], 3 + way)
            for way in range(2):
                send_w(0, lambda: sub0(0, 2), dev_z[way], zrecv0(way, 1, 3))
            pass_plane(0, 0)

        def hop_step(hop, s):
            for way in range(2):
                dz = (8 - hop) if way == 0 else hop
                half = (0, 1) if way == 0 else (2, 3)
                if hop == 4 and s not in half:
                    continue
                wait_w(sub0(dz, SUBS[s]), zrecv0(way, hop, s))
                if hop < 3 or (hop == 3 and s in half):
                    send_w(0, lambda dz=dz: sub0(dz, SUBS[s]), dev_z[way], zrecv0(way, hop + 1, s))
            if s == 3 and hop < 4:
                pass_plane(0, 2 * hop - 1)
                pass_plane(0, 2 * hop)
            if s == 3 and hop == 4:
                pass_plane(0, 7)

        yield first
        yield second
        yield third
        for hop in range(1, 4):
            for s in range(4):
                yield functools.partial(hop_step, hop, s)

        def last():
            for s in range(4):
                hop_step(4, s)

        yield last

    def ticks1():
        def zblock(dz):
            return wbuf.at[zs[dz], :, x, 1]

        def xrecv(n, kind, way):
            return 9 + n * 4 + kind * 2 + way

        def x1(n):
            for way in range(2):
                send_w(1, lambda: zblock(PLANES[n]), dev_x[way], xrecv(n, 0, way))

        def x2(n):
            dz = PLANES[n]
            for way, (dx, half) in enumerate(((3, 0), (1, 1))):
                wait_w(wbuf.at[zs[dz], :, xs[dx], 1], xrecv(n, 0, way))
                send_w(1, lambda dx=dx, half=half: wbuf.at[zs[dz], half, xs[dx], 1], dev_x[way], xrecv(n, 1, way))

        def done(n):
            for way in range(2):
                wait_w(wbuf.at[zs[PLANES[n]], way, xs[2], 1], xrecv(n, 1, way))
            pass_plane(1, n)

        def zhop(hop):
            for way in range(2):
                dz = (8 - hop) if way == 0 else hop
                if hop == 4:
                    wait_w(wbuf.at[zs[4], way, x, 1], 1 + way * 4 + 3)
                    continue
                wait_w(zblock(dz), 1 + way * 4 + hop - 1)

                def view(dz=dz, way=way):
                    return zblock(dz) if hop < 3 else wbuf.at[zs[dz], way, x, 1]

                send_w(1, view, dev_z[way], 1 + way * 4 + hop)

        def first():
            get_w.wait()
            w_first.wait_recv()
            for way in range(2):
                send_w(1, lambda: zblock(0), dev_z[way], 1 + way * 4)
            x1(0)

        plan = [
            [(zhop, 1), (x1, 1), (x1, 2)],
            [(x2, 0)],
            [(zhop, 2), (x1, 3), (x1, 4)],
            [(x2, 1), (x2, 2), (done, 0)],
            [(zhop, 3), (x1, 5), (x1, 6)],
            [(x2, 3)],
            [(done, 1), (done, 2), (zhop, 4), (x1, 7)],
            [(x2, 4)],
            [(x2, 5)],
            [(done, 3), (done, 4), (x2, 6)],
            [(x2, 7)],
            [(done, 5)],
            [(done, 6)],
            [(done, 7)],
            [],
        ]

        def run(steps):
            for step, value in steps:
                step(value)

        yield first
        for steps in plan:
            yield functools.partial(run, steps)

    zero_ticks, one_ticks = list(ticks0()), list(ticks1())
    assert len(zero_ticks) == len(one_ticks) == 16

    def tick(n):
        pl.when(core == 0)(zero_ticks[n])
        pl.when(core == 1)(one_ticks[n])

    get_lay.wait()
    first = ctx * 128
    starts, ends, sizes = lay[0:1, :], lay[1:2, :], lay[2:3, :]
    query = first + lax.broadcasted_iota(jnp.int32, (1, 128), 1)
    base = query & (-sizes)
    row = first + lax.broadcasted_iota(jnp.int32, (128, 128), 0)
    inside = (row >= starts) & (row < ends)
    bias[0, 0:128, :] = jnp.where(inside & (row < base), 0.0, NEG)
    bias[1, 0:128, :] = jnp.where(inside & (row < base + sizes), 0.0, NEG)
    bnoisy[...] = jnp.where(inside & (row >= base) & (row < base + sizes), 0.0, NEG)
    for slot in range(1, 8):
        far = jnp.where(row - slot * 128 >= starts, 0.0, NEG)
        bias[0, slot * 128:(slot + 1) * 128, :] = far
        bias[1, slot * 128:(slot + 1) * 128, :] = far

    tick(0)
    pltpu.make_async_copy(qs, qs, dsem.at[4]).wait()
    get_kv.wait()
    get_kn.wait()

    def lanes(group):
        return pl.ds(pl.multiple_of(group * 128, 128), 128)

    def keys_of(pair, kind, group):
        return kvw[2 * pair:2 * pair + 2, kind, :, lanes(group)].reshape(256, 128)

    @pl.loop(0, 4)
    def _(i):
        group = lax.div(i, 2)
        pb = group * 4 + lax.rem(i, 2)
        raw = nt(kvn[0, :, lanes(group)], qs[pb])
        masked = bnoisy[...]
        st[pb, 1024:1152, :] = raw + jnp.concatenate([masked, masked], 1)

    def score(pair):
        @pl.loop(0, 8)
        def _(pb):
            group = lax.div(pb, 4)
            raw = nt(keys_of(pair, 0, group), qs[pb])
            masked = bias[lax.div(lax.rem(pb, 4), 2), pair * 256:(pair + 1) * 256, :]
            st[pb, pair * 256:(pair + 1) * 256, :] = raw + jnp.concatenate([masked, masked], 1)

    tick(1)
    kv_pass(1)
    kv_odd(1)
    score(0)
    tick(2)
    kv_pass(2)
    kv_odd(3)
    tick(3)
    score(1)
    kv_pass(3)
    kv_odd(5)
    tick(4)
    score(2)
    tick(5)
    kv_odd(7)
    score(3)
    tick(6)

    def turned(value):
        return value.astype(F32).T.astype(BF16)

    for group in range(2):
        for slot in range(9):
            part = slice(slot * 128, (slot + 1) * 128)
            width = slice(group * 128, (group + 1) * 128)
            for kind, target in ((0, kt), (1, vt)):
                rows = kvn[kind, :, width] if slot == 8 else kvw[slot, kind, :, width]
                target[group, :, part] = turned(rows)
    tick(7)

    def softmax(copy_id, low, high):
        count = 9 if copy_id == 0 else 8

        @pl.loop(low, high)
        def _(i):
            group = lax.div(i, 2)
            pair = lax.rem(i, 2)
            pb = group * 4 + copy_id * 2 + pair
            peak = jnp.max(st[pb, 0:128 * count, :], axis=0, keepdims=True)
            total = jnp.zeros((1, 256), F32)
            for block in range(count):
                part = slice(block * 128, (block + 1) * 128)
                weight = jnp.exp2((st[pb, part, :] - peak) * EXP2)
                total = total + jnp.sum(weight, axis=0, keepdims=True)
                pt[pb, part, :] = weight.astype(BF16)
            inverse = 1.0 / total
            lrow[pb] = jnp.broadcast_to(inverse, (8, 256))
            lcol[pb] = jnp.broadcast_to(inverse, (128, 256)).T
            result = nn(vt[group, :, 0:128 * count], pt[pb, 0:128 * count, :]) * inverse
            for half in range(2):
                head = group * 4 + pair * 2 + half
                block = result[:, half * 128:(half + 1) * 128].T.astype(BF16)
                att[copy_id * 128:(copy_id + 1) * 128, lanes(head)] = block

    softmax(0, 0, 2)
    tick(8)
    softmax(0, 2, 4)
    tick(9)
    softmax(1, 0, 2)
    tick(10)
    softmax(1, 2, 4)
    tick(11)
    get_g.wait()

    def plane(n):
        for i in range(2):
            @pl.when(core == 1 - i)
            def _():
                passed(i, n).wait_recv()

        dz = PLANES[n]
        zz = zs[dz]
        lines = [wbuf[zz, line].reshape(256, 1024) for line in range(2)]
        at = pl.multiple_of(zz * 512, 512)
        rows = gbuf[:, :, pl.ds(at, 512)].reshape(256, 512)
        for piece in range(4):
            part = slice(piece * 256, (piece + 1) * 256)
            term = nn(rows[:, 0:256], lines[0][:, part]) + nn(rows[:, 256:512], lines[1][:, part])
            if n == 0:
                gacc[:, part] = term
            else:
                gacc[:, part] += term
        where = lax.rem(zz, 4)
        mine = lax.div(zz, 4) == hd
        for line in range(2):
            part = slice(line * 256, (line + 1) * 256)
            value = nt(att[...], lines[line])

            @pl.when(mine)
            def _():
                ypart[where, :, part] = value

            @pl.when(jnp.logical_not(mine))
            def _():
                ysend[where, :, part] = value.astype(BF16)

        @pl.when(jnp.logical_not(mine))
        def _():
            remote(ysend.at[where], yrecv.at[where], es.at[where], er.at[where], dev_head).start()

    for n in range(8):
        if n < 4:
            tick(12 + n)
        plane(n)

    @pl.loop(0, 8)
    def _(pb):
        group = lax.div(pb, 4)
        copy_id = lax.div(lax.rem(pb, 4), 2)
        pair = lax.rem(pb, 2)
        rows = pl.ds(pl.multiple_of(copy_id * 128, 128), 128)
        for half in range(2):
            part = slice(half * 128, (half + 1) * 128)
            head = group * 4 + pair * 2 + half
            grad = gacc[rows, lanes(head)].astype(BF16).astype(F32)
            product = grad * att[rows, lanes(head)].astype(F32)
            delta = jnp.sum(product.T, axis=0, keepdims=True)
            dl[pb, :, part] = jnp.broadcast_to(delta, (8, 128)) * lrow[pb, :, part]
            gs[pb, part, :] = (grad * lcol[pb, part, :]).astype(BF16)

    def grads(keys, values, where, size, group, blocks):
        dk = jnp.zeros((size, 128), F32)
        dv = jnp.zeros((size, 128), F32)
        for b in blocks:
            pb = group * 4 + b
            flow = nt(values, gs[pb])
            weight = pt[pb, where:where + size, :]
            dscore = (weight.astype(F32) * (flow - dl[pb, 0:1, :])).astype(BF16)
            dst[pb, where:where + size, :] = dscore
            dv = dv + nn(weight, gs[pb])
            dk = dk + nn(dscore, qs[pb])
        return dk * SCALE, dv

    def send_odd(pair):
        src = stage.at[pair]

        @pl.when(core == 0)
        def _():
            if pair == 3:
                remote(src, ret.at[3], rs.at[3 + pair], rr.at[3], dev_seven).start()
            else:
                remote(src, col.at[pair], rs.at[3 + pair], rr.at[4 + pair], dev_pair).start()

        @pl.when(core == 1)
        def _():
            if pair == 0:
                remote(src, ret.at[3], rs.at[3 + pair], rr.at[3], dev_pair).start()
            else:
                remote(src, col.at[pair - 1], rs.at[3 + pair], rr.at[3 + pair], dev_pair).start()

    def collect(k):
        remote(col.at[k - 1], col.at[k - 1], rs.at[0], rr.at[3 + k], dev_pair).wait_recv()
        comb[k - 1] = (evens[k - 1] + col[k - 1].astype(F32)).astype(BF16)
        remote(comb.at[k - 1], ret.at[k - 1], rs.at[k - 1], rr.at[k - 1], earlier[k]).start()

    for pair in (3, 2, 1, 0):
        @pl.loop(0, 2)
        def _(group):
            dk, dv = grads(
                keys_of(pair, 0, group), keys_of(pair, 1, group), pair * 256, 256, group, range(4)
            )
            for kind, value in ((0, dk), (1, dv)):
                if pair == 0:
                    own[kind, :, lanes(group)] = value[0:128]
                else:
                    evens[pair - 1, kind, :, lanes(group)] = value[0:128]
                stage[pair, kind, :, lanes(group)] = value[128:256].astype(BF16)

        send_odd(pair)
        if pair in (0, 1):
            collect(pair + 2)

    @pl.loop(0, 2)
    def _(group):
        dk, dv = grads(
            kvn[0, :, lanes(group)], kvn[1, :, lanes(group)], 1024, 128, group, range(2)
        )
        dkvv[0, 0, :, lanes(group)] = dk
        dkvv[1, 0, :, lanes(group)] = dv

    def dqueries(copy_id):
        count = 1152 if copy_id == 0 else 1024

        @pl.loop(0, 4)
        def _(i):
            group = lax.div(i, 2)
            pair = lax.rem(i, 2)
            pb = group * 4 + copy_id * 2 + pair
            result = nn(kt[group, :, 0:count], dst[pb, 0:count, :]) * SCALE
            for half in range(2):
                head = group * 4 + pair * 2 + half
                dqv[copy_id, :, lanes(head)] = result[:, half * 128:(half + 1) * 128].T

        return fetch(dqv.at[copy_id], dq_hbm.at[copy_id], dsem.at[6 + copy_id])

    collect(1)
    dq0 = dqueries(0)
    dq1 = dqueries(1)

    for j in range(4):
        remote(ysend.at[j], yrecv.at[j], es.at[j], er.at[j], dev_head).wait_recv()
        part = slice(j * 512, (j + 1) * 512)
        total = ypart[j] + yrecv[j].astype(F32)
        for copy_id in range(2):
            yout[copy_id, :, part] = total[copy_id * 128:(copy_id + 1) * 128].astype(BF16)
    put_y = fetch(yout, out_hbm, dsem.at[0])

    for n in range(4):
        remote(ret.at[n], ret.at[n], rs.at[n], rr.at[n], dev_pair).wait_recv()
    for kind in range(2):
        total = own[kind]
        for n in range(4):
            total = total + ret[n, kind].astype(F32)
        dkvv[kind, 1] = total
    put_kv = fetch(dkvv, dkv_hbm, dsem.at[1])

    for copy in kv_far:
        copy.wait_send()
    w_first.wait_send()
    for k in (1, 2, 3):
        remote(kvw.at[2 * k], kvw.at[2 * k], ks.at[3 + k], kr.at[0], dev_pair).wait_send()
    kv_own.wait_send()
    for i in range(2):
        @pl.when(core == i)
        def _():
            for n, view in enumerate(sent[i]):
                remote(view(), view(), ws.at[n + 1], wr.at[0], dev_y).wait_send()
            for n in range(8):
                passed(i, n).wait_send()

    for j in range(4):
        remote(ysend.at[j], yrecv.at[j], es.at[j], er.at[j], dev_head).wait_send()
    for n in range(7):
        remote(stage.at[0], stage.at[0], rs.at[n], rr.at[0], dev_pair).wait_send()
    for copy in (dq0, dq1, put_y, put_kv):
        copy.wait()


def per_device(queries, keys_values, grad_layer, out_proj, doc_layout):
    vm = pltpu.VMEM
    dma = pltpu.SemaphoreType.DMA
    scratch = [
        vm((NZ, NY, NX, 2, 32, 1024), BF16),
        vm((8, 256, 128), BF16),
        vm((8, 2, 128, 256), BF16),
        vm((2, 128, 256), BF16),
        vm((2, 128, 4096), BF16),
        vm((3, 128), jnp.int32),
        vm((2, 1024, 128), F32),
        vm((128, 128), F32),
        vm((8, 1152, 256), F32),
        vm((8, 1152, 256), BF16),
        vm((8, 1152, 256), BF16),
        vm((2, 128, 1152), BF16),
        vm((2, 128, 1152), BF16),
        vm((256, 1024), BF16),
        vm((256, 1024), F32),
        vm((8, 8, 256), F32),
        vm((8, 256, 128), F32),
        vm((8, 256, 128), BF16),
        vm((8, 8, 256), F32),
        vm((4, 256, 512), F32),
        vm((4, 256, 512), BF16),
        vm((4, 256, 512), BF16),
        vm((2, 128, 2048), BF16),
        vm((4, 2, 128, 256), BF16),
        vm((3, 2, 128, 256), F32),
        vm((3, 2, 128, 256), BF16),
        vm((3, 2, 128, 256), BF16),
        vm((4, 2, 128, 256), BF16),
        vm((2, 128, 256), F32),
        vm((2, 128, 1024), F32),
        vm((2, 2, 128, 256), F32),
        dma((8,)), dma((8,)), dma((8,)), dma((48,)), dma((48,)),
        dma((8,)), dma((8,)), dma((4,)), dma((4,)), dma((8,)), dma((8,)),
    ]
    anywhere = pl.BlockSpec(memory_space=pl.ANY)
    return pl.pallas_call(
        kernel,
        out_shape=(
            jax.ShapeDtypeStruct((2, 128, 2048), BF16),
            jax.ShapeDtypeStruct((2, 128, 1024), F32),
            jax.ShapeDtypeStruct((2, 2, 128, 256), F32),
        ),
        in_specs=[anywhere] * 5,
        out_specs=(anywhere,) * 3,
        scratch_shapes=scratch,
        compiler_params=pltpu.CompilerParams(
            collective_id=0, has_side_effects=True, vmem_limit_bytes=62 * 1024 * 1024
        ),
    )(queries, keys_values, grad_layer, out_proj, doc_layout)


def solution(mesh):
    return jax.shard_map(
        per_device,
        mesh=mesh,
        in_specs=(
            P(None, "ctx", "head"),
            P(None, None, "ctx", "head"),
            P(None, "ctx", None),
            P("ctx", "head"),
            P(None, "ctx"),
        ),
        out_specs=(P(None, "ctx", "head"), P(None, "ctx", "head"), P(None, None, "ctx", "head")),
        check_vma=False,
    )
```

```python
import functools
import math

import jax
import jax.numpy as jnp
from jax import lax
from jax.experimental import pallas as pl
from jax.experimental.pallas import tpu as pltpu
from jax.sharding import PartitionSpec as P

F32 = jnp.float32
BF16 = jnp.bfloat16
MESH = pl.DeviceIdType.MESH
NEG = -1e30
SCALE = 128 ** -0.5
EXP2 = SCALE * math.log2(math.e)

NZ, NY, NX = 8, 2, 4
SUBS = (0, 3, 1, 2)
PLANES = (0, 7, 1, 6, 2, 5, 3, 4)


def nt(a, b):
    return lax.dot_general(a, b, (((1,), (1,)), ((), ())), preferred_element_type=F32)


def nn(a, b):
    return lax.dot_general(a, b, (((1,), (0,)), ((), ())), preferred_element_type=F32)


def kernel(
    q_hbm, kv_hbm, g_hbm, w_hbm, lay_hbm,
    out_hbm, dq_hbm, dkv_hbm,
    wbuf, qs, kvw, kvp, kvn, gbuf, lay, bias, bnoisy, st, pt, dst, vt, kt,
    att, gacc, lrow, lcol, gs, dl, ypart, ysend, yrecv, yout,
    stage, evens, col, comb, ret, back, retp, own, dqv, dkvv,
    dsem, ks, kr, ws, wr, pps, ppr, es, er, rs, rr,
):
    ctx = lax.axis_index("ctx")
    hd = lax.axis_index("head")
    core = lax.rem(ctx, 2)
    x = lax.rem(lax.div(ctx, 2), NX)
    yh = lax.rem(lax.div(ctx, 8), NY)
    z = lax.div(ctx, 16)

    def place(z_, y_, x_):
        return ((z_ * NY + y_) * NX + x_) * 2 + core

    xs = [lax.rem(x + d, NX) for d in range(NX)]
    zs = [lax.rem(z + d, NZ) for d in range(NZ)]
    dev_y = (place(z, 1 - yh, x), hd)
    dev_x = [(place(z, yh, xs[1]), hd), (place(z, yh, xs[3]), hd)]
    dev_z = [(place(zs[1], yh, x), hd), (place(zs[7], yh, x), hd)]
    dev_pair = (ctx + 1 - 2 * core, hd)
    dev_head = (ctx, 1 - hd)
    line = [(place(z, yh, xs[k]), hd) for k in range(NX)]
    dev_after = (lax.rem(ctx + 8, 128), hd)
    dev_prior = (lax.rem(ctx + 126, 128), hd)
    dev_follow = (lax.rem(ctx + 2, 128), hd)
    dev_before = (lax.rem(ctx + 120, 128), hd)

    def remote(src, dst_ref, send, recv, device):
        return pltpu.make_async_remote_copy(
            src_ref=src, dst_ref=dst_ref, send_sem=send, recv_sem=recv,
            device_id=device, device_id_type=MESH,
        )

    def fetch(src, dst_ref, sem):
        copy = pltpu.make_async_copy(src, dst_ref, sem)
        copy.start()
        return copy

    get_w = fetch(w_hbm, wbuf.at[z, yh, x, core], dsem.at[0])
    get_kv = fetch(kv_hbm.at[:, 1], kvw.at[0], dsem.at[1])
    get_kn = fetch(kv_hbm.at[:, 0], kvn, dsem.at[2])
    get_lay = fetch(lay_hbm, lay, dsem.at[3])
    for copy_id in range(2):
        for head in range(8):
            pb = (head // 4) * 4 + copy_id * 2 + (head % 4) // 2
            fetch(
                q_hbm.at[copy_id, :, pl.ds(head * 128, 128)],
                qs.at[pb, pl.ds((head % 2) * 128, 128)],
                dsem.at[4],
            )
    get_g = fetch(g_hbm, gbuf, dsem.at[5])

    barrier = pltpu.get_barrier_semaphore()
    planar = [(place(z, 1 - yh, xs[k]), hd) for k in range(NX)]
    meet = [*planar, *line[1:], *dev_z, dev_pair, dev_head, dev_after, dev_before, dev_prior, dev_follow]
    for device in meet:
        pl.semaphore_signal(barrier, inc=1, device_id=device, device_id_type=MESH)
    pl.semaphore_wait(barrier, len(meet))

    own_kv = kv_hbm.at[:, 1]
    kv_next = remote(own_kv, kvp, ks.at[7], kr.at[0], dev_after)

    def kv_start():
        kv_next.start()

        @pl.when(core == 0)
        def _():
            remote(own_kv, kvw.at[1], ks.at[0], kr.at[1], dev_pair).start()

    def kv_line():
        for k in (1, 2, 3):
            @pl.when(x + k < NX)
            def _():
                remote(own_kv, kvw.at[2 * k], ks.at[k], kr.at[2 * k], line[k]).start()

    def kv_before():
        kv_next.wait_recv()
        for k in (1, 2, 3):
            @pl.when(x + k >= NX)
            def _():
                remote(kvp, kvw.at[2 * k], ks.at[k], kr.at[2 * k], line[k]).start()

        @pl.when(core == 1)
        def _():
            remote(kvp, kvw.at[7], ks.at[0], kr.at[7], dev_pair).start()

    def kv_pass(k):
        remote(kvp, kvw.at[2 * k], ks.at[k], kr.at[2 * k], line[k]).wait_recv()

        @pl.when(core == 0)
        def _():
            remote(
                kvw.at[2 * k], kvw.at[2 * k + 1], ks.at[3 + k], kr.at[2 * k + 1], dev_pair
            ).start()

        @pl.when(core == 1)
        def _():
            remote(
                kvw.at[2 * k], kvw.at[2 * k - 1], ks.at[3 + k], kr.at[2 * k - 1], dev_pair
            ).start()

    def kv_odd(slot):
        remote(kvw.at[slot], kvw.at[slot], ks.at[0], kr.at[slot], dev_pair).wait_recv()

    sent = ([], [])

    def send_w(core_id, view, device, recv, source=None):
        n = len(sent[core_id])
        target = view()
        src = target if source is None else source
        remote(src, target, ws.at[n], wr.at[recv], device).start()
        sent[core_id].append(view)

    def wait_w(src, recv):
        remote(src, src, ws.at[0], wr.at[recv], dev_y).wait_recv()

    def passed(core_id, n):
        src = wbuf.at[zs[PLANES[n]], :, :, core_id]
        return remote(src, src, pps.at[n], ppr.at[n], dev_pair)

    def pass_plane(core_id, n):
        passed(core_id, n).start()

    low = lax.rem(lax.div(x, 2) * 2, NX)
    high = lax.rem(low + 2, NX)
    mate = low + 1 - lax.rem(x, 2)
    across = 1 - yh

    def sub0(dz, sub):
        row = yh if sub < 2 else across
        return wbuf.at[zs[dz], row, pl.ds(low if sub % 2 == 0 else high, 2), 0]

    def zrecv0(way, hop, sub):
        return 6 + (way * 4 + hop - 1) * 4 + sub

    def away(way, hop):
        return (8 - hop) % 8 if way == 0 else hop

    def near(k):
        row = yh if k < NX else across
        return wbuf.at[z, row, xs[k % NX], 0]

    def ticks0():
        def start(*steps):
            for k in steps:
                device = line[k] if k < NX else (place(z, across, xs[k % NX]), hd)
                send_w(0, lambda: near(0), device, 38 + k, w_hbm)

        def start_z():
            for way in range(2):
                send_w(0, lambda: near(0), dev_z[way], zrecv0(way, 1, 0), w_hbm)

        def shard_at(row, col):
            return wbuf.at[z, row, col, 0]

        def arrive(k):
            row = yh if k < NX else across
            wait_w(wbuf.at[z, row, xs[(NX - k % NX) % NX], 0], 38 + k)

        def all_near():
            for k in range(2, 8):
                if k != 3:
                    arrive(k)
            for sub in range(1, 4):
                zhop(sub, 0)

        def mate_first():
            get_w.wait()
            for k in (1, 3):
                arrive(k)
            for way in range(2):
                send_w(0, lambda: shard_at(yh, mate), dev_z[way], zrecv0(way, 1, 0))

        def zhop(sub, hop):
            for way in range(2):
                half = sub < 2 if way == 0 else sub >= 2
                if hop > 0:
                    if hop == 4 and not half:
                        continue
                    wait_w(sub0(away(way, hop), sub), zrecv0(way, hop, sub))
                if hop < 3 or (hop == 3 and half):
                    send_w(0, lambda way=way: sub0(away(way, hop), sub), dev_z[way],
                           zrecv0(way, hop + 1, sub))

        def give(*planes):
            for n in planes:
                pass_plane(0, n)

        plan = [
            [(start_z,), (start, 1, 3)],
            [(mate_first,)],
            [(all_near,)],
            [(zhop, 0, 1)],
            [(zhop, 1, 1), (zhop, 2, 1), (give, 0)],
            [(zhop, 3, 1), (zhop, 0, 2)],
            [(zhop, 1, 2), (give, 1, 2)],
            [(zhop, 2, 2)],
            [(zhop, 3, 2)],
            [(zhop, 0, 3), (zhop, 1, 3), (give, 3, 4)],
            [(zhop, 2, 3)],
            [(zhop, 3, 3)],
            [(give, 5, 6), (zhop, 0, 4), (zhop, 1, 4)],
            [],
            [(zhop, 2, 4), (zhop, 3, 4), (give, 7)],
            [], [], [],
            [(start, 4, 2, 5, 7, 6)],
        ]
        return [functools.partial(run, steps) for steps in plan]

    def run(steps):
        for step, *values in steps:
            step(*values)

    def ticks1():
        def shard(n, other):
            return wbuf.at[zs[PLANES[n]], across if other else yh, x, 1]

        def beside(n, other, dx):
            return wbuf.at[zs[PLANES[n]], across if other else yh, xs[dx], 1]

        def xrecv(n, other, way):
            return 16 + n * 6 + other * 3 + way

        def yout(*planes):
            for n in planes:
                local = {"source": w_hbm} if n == 0 else {}
                send_w(1, lambda n=n: shard(n, 0), dev_y, 8 + n, **local)

        def xout(*planes):
            for n in planes:
                local = {"source": w_hbm} if n == 0 else {}
                for way in range(2):
                    send_w(1, lambda n=n: shard(n, 0), dev_x[way], xrecv(n, 0, way), **local)

        def turn(*planes):
            for n in planes:
                wait_w(shard(n, 1), 8 + n)
                for way in range(2):
                    send_w(1, lambda n=n: shard(n, 1), dev_x[way], xrecv(n, 1, way))

        def onward(other, *planes):
            for n in planes:
                for way, dx in enumerate((3, 1)):
                    wait_w(beside(n, other, dx), xrecv(n, other, way))
                dx = 1 if other else 3
                send_w(1, lambda n=n: beside(n, other, dx), dev_x[other], xrecv(n, other, 2))

        def give(*planes):
            for n in planes:
                for other in range(2):
                    wait_w(beside(n, other, 2), xrecv(n, other, 2))
                pass_plane(1, n)

        def half(dz, way):
            return wbuf.at[zs[dz], yh, x, 1, pl.ds(16 * way, 16)]

        def zhop(hop):
            for way in range(2):
                dz = away(way, hop)
                if hop == 4:
                    wait_w(half(4, way), way * 4 + 3)
                    continue
                if hop > 0:
                    wait_w(wbuf.at[zs[dz], yh, x, 1], way * 4 + hop - 1)

                def view(dz=dz, way=way):
                    return half(dz, way) if hop == 3 else wbuf.at[zs[dz], yh, x, 1]

                local = {"source": w_hbm} if hop == 0 else {}
                send_w(1, view, dev_z[way], way * 4 + hop, **local)

        plan = [
            [(zhop, 0), (yout, 0)],
            [(zhop, 1), (yout, 1, 2)],
            [(zhop, 2), (yout, 3, 4), (xout, 0, 1, 2)],
            [(zhop, 3), (yout, 5, 6), (turn, 0, 1, 2), (xout, 3, 4)],
            [(zhop, 4), (yout, 7), (onward, 0, 0, 1, 2), (turn, 3, 4), (xout, 5, 6), (onward, 1, 0, 1, 2)],
            [(onward, 0, 3, 4), (turn, 5, 6), (xout, 7), (get_w.wait,), (give, 0)],
            [(onward, 1, 3, 4), (turn, 7), (give, 1, 2)],
            [(onward, 0, 5, 6)],
            [(onward, 1, 5, 6)],
            [(onward, 0, 7), (give, 3, 4)],
            [(onward, 1, 7)],
            [],
            [(give, 5, 6)],
            [],
            [(give, 7)],
            [], [], [], [],
        ]
        return [functools.partial(run, steps) for steps in plan]

    zero_ticks, one_ticks = ticks0(), ticks1()
    assert len(zero_ticks) == len(one_ticks) == 19

    def tick(n):
        pl.when(core == 0)(zero_ticks[n])
        pl.when(core == 1)(one_ticks[n])

    tick(0)
    kv_start()
    tick(18)
    kv_line()

    get_lay.wait()
    first = ctx * 128
    starts, ends, sizes = lay[0:1, :], lay[1:2, :], lay[2:3, :]
    query = first + lax.broadcasted_iota(jnp.int32, (1, 128), 1)
    base = query & (-sizes)
    row = first + lax.broadcasted_iota(jnp.int32, (128, 128), 0)
    inside = (row >= starts) & (row < ends)
    bias[0, 0:128, :] = jnp.where(inside & (row < base), 0.0, NEG)
    bias[1, 0:128, :] = jnp.where(inside & (row < base + sizes), 0.0, NEG)
    bnoisy[...] = jnp.where(inside & (row >= base) & (row < base + sizes), 0.0, NEG)
    for slot in range(1, 8):
        far = jnp.where(row - slot * 128 >= starts, 0.0, NEG)
        bias[0, slot * 128:(slot + 1) * 128, :] = far
        bias[1, slot * 128:(slot + 1) * 128, :] = far

    pltpu.make_async_copy(qs, qs, dsem.at[4]).wait()
    get_kv.wait()
    get_kn.wait()

    def lanes(group):
        return pl.ds(pl.multiple_of(group * 128, 128), 128)

    def keys_of(pair, kind, group):
        return kvw[2 * pair:2 * pair + 2, kind, :, lanes(group)].reshape(256, 128)

    @pl.loop(0, 4)
    def _(i):
        group = lax.div(i, 2)
        pb = group * 4 + lax.rem(i, 2)
        raw = nt(kvn[0, :, lanes(group)], qs[pb])
        masked = bnoisy[...]
        st[pb, 1024:1152, :] = raw + jnp.concatenate([masked, masked], 1)

    def score(pair):
        @pl.loop(0, 8, unroll=4)
        def _(pb):
            group = lax.div(pb, 4)
            raw = nt(keys_of(pair, 0, group), qs[pb])
            masked = bias[lax.div(lax.rem(pb, 4), 2), pair * 256:(pair + 1) * 256, :]
            st[pb, pair * 256:(pair + 1) * 256, :] = raw + jnp.concatenate([masked, masked], 1)

    tick(1)
    kv_before()
    tick(2)
    tick(3)
    kv_pass(1)
    kv_odd(1)
    score(0)
    kv_pass(2)
    kv_odd(3)
    score(1)
    kv_pass(3)
    tick(4)
    kv_odd(5)
    score(2)
    kv_odd(7)
    score(3)
    tick(5)

    def turned(value):
        return value.astype(F32).T.astype(BF16)

    for group in range(2):
        for slot in range(9):
            part = slice(slot * 128, (slot + 1) * 128)
            width = slice(group * 128, (group + 1) * 128)
            for kind, target in ((0, kt), (1, vt)):
                rows = kvn[kind, :, width] if slot == 8 else kvw[slot, kind, :, width]
                target[group, :, part] = turned(rows)


    def softmax(copy_id, low, high):
        count = 9 if copy_id == 0 else 8

        @pl.loop(low, high, unroll=2)
        def _(i):
            group = lax.div(i, 2)
            pair = lax.rem(i, 2)
            pb = group * 4 + copy_id * 2 + pair
            peak = jnp.max(st[pb, 0:128 * count, :], axis=0, keepdims=True)
            total = jnp.zeros((1, 256), F32)
            for block in range(count):
                part = slice(block * 128, (block + 1) * 128)
                weight = jnp.exp2((st[pb, part, :] - peak) * EXP2)
                total = total + jnp.sum(weight, axis=0, keepdims=True)
                pt[pb, part, :] = weight.astype(BF16)
            inverse = 1.0 / total
            lrow[pb] = jnp.broadcast_to(inverse, (8, 256))
            lcol[pb] = jnp.broadcast_to(inverse, (128, 256)).T
            result = nn(vt[group, :, 0:128 * count], pt[pb, 0:128 * count, :]) * inverse
            for half in range(2):
                head = group * 4 + pair * 2 + half
                block = result[:, half * 128:(half + 1) * 128].T.astype(BF16)
                att[copy_id * 128:(copy_id + 1) * 128, lanes(head)] = block

    softmax(1, 0, 2)
    softmax(1, 2, 4)
    tick(6)
    softmax(0, 0, 2)
    softmax(0, 2, 4)
    get_g.wait()

    def plane(n):
        for i in range(2):
            @pl.when(core == 1 - i)
            def _():
                passed(i, n).wait_recv()

        dz = PLANES[n]
        zz = zs[dz]
        lines = [wbuf[zz, line].reshape(256, 1024) for line in range(2)]
        at = pl.multiple_of(zz * 512, 512)
        where = lax.rem(zz, 4)

        @pl.when(lax.div(zz, 4) != hd)
        def _():
            for line in range(2):
                value = nt(att[...], wbuf[zz, line].reshape(256, 1024))
                ysend[where, :, line * 256:(line + 1) * 256] = value.astype(BF16)
            remote(ysend.at[where], yrecv.at[where], es.at[where], er.at[where], dev_head).start()

        rows = gbuf[:, :, pl.ds(at, 512)].reshape(256, 512)
        for piece in range(4):
            part = slice(piece * 256, (piece + 1) * 256)
            term = nn(rows[:, 0:256], lines[0][:, part]) + nn(rows[:, 256:512], lines[1][:, part])
            if n == 0:
                gacc[:, part] = term
            else:
                gacc[:, part] += term

    for n in range(8):
        tick(7 + n)
        plane(n)

    @pl.loop(0, 8, unroll=2)
    def _(pb):
        group = lax.div(pb, 4)
        copy_id = lax.div(lax.rem(pb, 4), 2)
        pair = lax.rem(pb, 2)
        rows = pl.ds(pl.multiple_of(copy_id * 128, 128), 128)
        for half in range(2):
            part = slice(half * 128, (half + 1) * 128)
            head = group * 4 + pair * 2 + half
            grad = gacc[rows, lanes(head)].astype(BF16).astype(F32)
            product = grad * att[rows, lanes(head)].astype(F32)
            delta = jnp.sum(product.T, axis=0, keepdims=True)
            dl[pb, :, part] = jnp.broadcast_to(delta, (8, 128)) * lrow[pb, :, part]
            gs[pb, part, :] = (grad * lcol[pb, part, :]).astype(BF16)

    def grads(keys, values, where, size, group, blocks):
        dk = jnp.zeros((size, 128), F32)
        dv = jnp.zeros((size, 128), F32)
        for b in blocks:
            pb = group * 4 + b
            flow = nt(values, gs[pb])
            weight = pt[pb, where:where + size, :]
            dscore = (weight.astype(F32) * (flow - dl[pb, 0:1, :])).astype(BF16)
            dst[pb, where:where + size, :] = dscore
            dv = dv + nn(weight, gs[pb])
            dk = dk + nn(dscore, qs[pb])
        return dk * SCALE, dv

    def send_odd(pair):
        src = stage.at[pair]

        @pl.when(core == 0)
        def _():
            if pair == 3:
                remote(src, ret.at[3], rs.at[3 + pair], rr.at[3], dev_pair).start()
            else:
                remote(src, col.at[pair], rs.at[3 + pair], rr.at[4 + pair], dev_pair).start()

        @pl.when(core == 1)
        def _():
            if pair == 0:
                remote(src, ret.at[3], rs.at[3 + pair], rr.at[3], dev_pair).start()
            else:
                remote(src, col.at[pair - 1], rs.at[3 + pair], rr.at[3 + pair], dev_pair).start()

    def collect(k):
        remote(col.at[k - 1], col.at[k - 1], rs.at[0], rr.at[3 + k], dev_pair).wait_recv()
        comb[k - 1] = (evens[k - 1] + col[k - 1].astype(F32)).astype(BF16)
        remote(comb.at[k - 1], ret.at[k - 1], rs.at[k - 1], rr.at[k - 1], line[NX - k] if k > 1 else dev_prior).start()

    for pair in (3, 2, 1, 0):
        @pl.loop(0, 2, unroll=2)
        def _(group):
            dk, dv = grads(
                keys_of(pair, 0, group), keys_of(pair, 1, group), pair * 256, 256, group, range(4)
            )
            for kind, value in ((0, dk), (1, dv)):
                if pair == 0:
                    own[kind, :, lanes(group)] = value[0:128]
                else:
                    evens[pair - 1, kind, :, lanes(group)] = value[0:128]
                stage[pair, kind, :, lanes(group)] = value[128:256].astype(BF16)

        send_odd(pair)
        if pair < 3:
            @pl.when(core == 0)
            def _():
                collect(pair + 1)
        if pair < 2:
            @pl.when(core == 1)
            def _():
                collect(pair + 2)

    @pl.loop(0, 2)
    def _(group):
        dk, dv = grads(
            kvn[0, :, lanes(group)], kvn[1, :, lanes(group)], 1024, 128, group, range(2)
        )
        dkvv[0, 0, :, lanes(group)] = dk
        dkvv[1, 0, :, lanes(group)] = dv

    def dqueries(copy_id):
        count = 1152 if copy_id == 0 else 1024

        @pl.loop(0, 4, unroll=2)
        def _(i):
            group = lax.div(i, 2)
            pair = lax.rem(i, 2)
            pb = group * 4 + copy_id * 2 + pair
            result = nn(kt[group, :, 0:count], dst[pb, 0:count, :]) * SCALE
            for half in range(2):
                head = group * 4 + pair * 2 + half
                dqv[copy_id, :, lanes(head)] = result[:, half * 128:(half + 1) * 128].T

        return fetch(dqv.at[copy_id], dq_hbm.at[copy_id], dsem.at[6 + copy_id])

    pl.when(core == 1)(functools.partial(collect, 1))
    dq0 = dqueries(0)

    def line_sums():
        for n in (2, 1, 3):
            remote(ret.at[n], ret.at[n], rs.at[n], rr.at[n], dev_pair).wait_recv()
        for kind in range(2):
            mine, other = own[kind], jnp.zeros((128, 256), F32)
            for n in (1, 2, 3):
                here = core == 0 if n == 3 else x + n + 1 < NX
                value = ret[n, kind].astype(F32)
                mine = mine + jnp.where(here, value, 0.0)
                other = other + jnp.where(here, 0.0, value)
            own[kind] = mine
            back[kind] = other.astype(BF16)
        remote(back, retp, rs.at[7], rr.at[7], dev_before).start()

    line_sums()
    dq1 = dqueries(1)

    def mine(j):
        for line_id in range(2):
            part = slice(line_id * 256, (line_id + 1) * 256)
            ypart[j, :, part] = nt(att[...], wbuf[hd * 4 + j, line_id].reshape(256, 1024))

    for j in range(4):
        mine(j)

    def finish(j):
        remote(ysend.at[j], yrecv.at[j], es.at[j], er.at[j], dev_head).wait_recv()
        part = slice(j * 512, (j + 1) * 512)
        total = ypart[j] + yrecv[j].astype(F32)
        for copy_id in range(2):
            yout[copy_id, :, part] = total[copy_id * 128:(copy_id + 1) * 128].astype(BF16)

    for j in range(4):
        finish(j)
    put_y = fetch(yout, out_hbm, dsem.at[0])

    def last_sum():
        remote(ret.at[0], ret.at[0], rs.at[0], rr.at[0], dev_pair).wait_recv()
        remote(back, retp, rs.at[7], rr.at[7], dev_before).wait_recv()
        for kind in range(2):
            dkvv[kind, 1] = own[kind] + ret[0, kind].astype(F32) + retp[kind].astype(F32)

    last_sum()
    put_kv = fetch(dkvv, dkv_hbm, dsem.at[1])

    for n in range(8):
        remote(own_kv, kvp, ks.at[n], kr.at[0], dev_after).wait_send()
    for i in range(2):
        @pl.when(core == i)
        def _():
            for n, view in enumerate(sent[i]):
                remote(view(), view(), ws.at[n], wr.at[0], dev_y).wait_send()
            for n in range(8):
                passed(i, n).wait_send()

    for j in range(4):
        remote(ysend.at[j], yrecv.at[j], es.at[j], er.at[j], dev_head).wait_send()
    for n in range(8):
        remote(stage.at[0], stage.at[0], rs.at[n], rr.at[0], dev_pair).wait_send()
    for copy in (dq0, dq1, put_y, put_kv):
        copy.wait()


def per_device(queries, keys_values, grad_layer, out_proj, doc_layout):
    vm = pltpu.VMEM
    dma = pltpu.SemaphoreType.DMA
    scratch = [
        vm((NZ, NY, NX, 2, 32, 1024), BF16),
        vm((8, 256, 128), BF16),
        vm((8, 2, 128, 256), BF16),
        vm((2, 128, 256), BF16),
        vm((2, 128, 256), BF16),
        vm((2, 128, 4096), BF16),
        vm((3, 128), jnp.int32),
        vm((2, 1024, 128), F32),
        vm((128, 128), F32),
        vm((8, 1152, 256), F32),
        vm((8, 1152, 256), BF16),
        vm((8, 1152, 256), BF16),
        vm((2, 128, 1152), BF16),
        vm((2, 128, 1152), BF16),
        vm((256, 1024), BF16),
        vm((256, 1024), F32),
        vm((8, 8, 256), F32),
        vm((8, 256, 128), F32),
        vm((8, 256, 128), BF16),
        vm((8, 8, 256), F32),
        vm((4, 256, 512), F32),
        vm((4, 256, 512), BF16),
        vm((4, 256, 512), BF16),
        vm((2, 128, 2048), BF16),
        vm((4, 2, 128, 256), BF16),
        vm((3, 2, 128, 256), F32),
        vm((3, 2, 128, 256), BF16),
        vm((3, 2, 128, 256), BF16),
        vm((4, 2, 128, 256), BF16),
        vm((2, 128, 256), BF16),
        vm((2, 128, 256), BF16),
        vm((2, 128, 256), F32),
        vm((2, 128, 1024), F32),
        vm((2, 2, 128, 256), F32),
        dma((8,)), dma((8,)), dma((8,)), dma((72,)), dma((72,)),
        dma((8,)), dma((8,)), dma((4,)), dma((4,)), dma((8,)), dma((8,)),
    ]
    anywhere = pl.BlockSpec(memory_space=pl.ANY)
    return pl.pallas_call(
        kernel,
        out_shape=(
            jax.ShapeDtypeStruct((2, 128, 2048), BF16),
            jax.ShapeDtypeStruct((2, 128, 1024), F32),
            jax.ShapeDtypeStruct((2, 2, 128, 256), F32),
        ),
        in_specs=[anywhere] * 5,
        out_specs=(anywhere,) * 3,
        scratch_shapes=scratch,
        compiler_params=pltpu.CompilerParams(
            collective_id=0, has_side_effects=True, vmem_limit_bytes=62 * 1024 * 1024
        ),
    )(queries, keys_values, grad_layer, out_proj, doc_layout)


def solution(mesh):
    return jax.shard_map(
        per_device,
        mesh=mesh,
        in_specs=(
            P(None, "ctx", "head"),
            P(None, None, "ctx", "head"),
            P(None, "ctx", None),
            P("ctx", "head"),
            P(None, "ctx"),
        ),
        out_specs=(P(None, "ctx", "head"), P(None, "ctx", "head"), P(None, None, "ctx", "head")),
        check_vma=False,
    )
```

```python
import functools
import math

import jax
import jax.numpy as jnp
from jax import lax
from jax.experimental import pallas as pl
from jax.experimental.pallas import tpu as pltpu
from jax.sharding import PartitionSpec as P

F32 = jnp.float32
BF16 = jnp.bfloat16
MESH = pl.DeviceIdType.MESH
NEG = -1e30
SCALE = 128 ** -0.5
EXP2 = SCALE * math.log2(math.e)

NZ, NY, NX = 8, 2, 4
SUBS = (0, 3, 1, 2)
PLANES = (0, 7, 1, 6, 2, 5, 3, 4)


def nt(a, b):
    return lax.dot_general(a, b, (((1,), (1,)), ((), ())), preferred_element_type=F32)


def nn(a, b):
    return lax.dot_general(a, b, (((1,), (0,)), ((), ())), preferred_element_type=F32)


def kernel(
    q_hbm, kv_hbm, g_hbm, w_hbm, lay_hbm,
    yout, dqv, dkvv,
    wbuf, qs, kvw, kvp, kvn, gbuf, lay, bias, bnoisy, st, pt, dst, vt, kt,
    att, gacc, lrow, lcol, gs, dl, ypart, ysend, yrecv,
    stage, evens, col, comb, ret, back, retp, own,
    dsem, ks, kr, ws, wr, pps, ppr, es, er, rs, rr,
):
    ctx = lax.axis_index("ctx")
    hd = lax.axis_index("head")
    core = lax.rem(ctx, 2)
    x = lax.rem(lax.div(ctx, 2), NX)
    yh = lax.rem(lax.div(ctx, 8), NY)
    z = lax.div(ctx, 16)

    def place(z_, y_, x_):
        return ((z_ * NY + y_) * NX + x_) * 2 + core

    xs = [lax.rem(x + d, NX) for d in range(NX)]
    zs = [lax.rem(z + d, NZ) for d in range(NZ)]
    dev_y = (place(z, 1 - yh, x), hd)
    dev_x = [(place(z, yh, xs[1]), hd), (place(z, yh, xs[3]), hd)]
    dev_z = [(place(zs[1], yh, x), hd), (place(zs[7], yh, x), hd)]
    dev_pair = (ctx + 1 - 2 * core, hd)
    dev_head = (ctx, 1 - hd)
    line = [(place(z, yh, xs[k]), hd) for k in range(NX)]
    dev_after = (lax.rem(ctx + 8, 128), hd)
    dev_before = (lax.rem(ctx + 120, 128), hd)

    def remote(src, dst_ref, send, recv, device):
        return pltpu.make_async_remote_copy(
            src_ref=src, dst_ref=dst_ref, send_sem=send, recv_sem=recv,
            device_id=device, device_id_type=MESH,
        )

    def fetch(src, dst_ref, sem):
        copy = pltpu.make_async_copy(src, dst_ref, sem)
        copy.start()
        return copy

    get_w = fetch(w_hbm, wbuf.at[z, yh, x, core], dsem.at[0])
    get_kv = fetch(kv_hbm.at[:, 1], kvw.at[0], dsem.at[1])
    get_kn = fetch(kv_hbm.at[:, 0], kvn, dsem.at[2])
    get_lay = fetch(lay_hbm, lay, dsem.at[3])
    for copy_id in range(2):
        for head in range(8):
            pb = (head // 4) * 4 + copy_id * 2 + (head % 4) // 2
            fetch(
                q_hbm.at[copy_id, :, pl.ds(head * 128, 128)],
                qs.at[pb, pl.ds((head % 2) * 128, 128)],
                dsem.at[4],
            )
    get_g = fetch(g_hbm, gbuf, dsem.at[5])

    barrier = pltpu.get_barrier_semaphore()
    planar = [(place(z, 1 - yh, xs[k]), hd) for k in range(NX)]
    meet = [*planar, *line[1:], *dev_z, dev_pair, dev_head, dev_after, dev_before]
    for device in meet:
        pl.semaphore_signal(barrier, inc=1, device_id=device, device_id_type=MESH)
    pl.semaphore_wait(barrier, len(meet))

    own_kv = kv_hbm.at[:, 1]
    kv_next = remote(own_kv, kvp, ks.at[7], kr.at[0], dev_after)

    def kv_start():
        kv_next.start()

        @pl.when(core == 0)
        def _():
            remote(own_kv, kvw.at[1], ks.at[0], kr.at[1], dev_pair).start()

    def kv_line():
        for k in (1, 2, 3):
            @pl.when(x + k < NX)
            def _():
                remote(own_kv, kvw.at[2 * k], ks.at[k], kr.at[2 * k], line[k]).start()

    def kv_before():
        kv_next.wait_recv()
        for k in (1, 2, 3):
            @pl.when(x + k >= NX)
            def _():
                remote(kvp, kvw.at[2 * k], ks.at[k], kr.at[2 * k], line[k]).start()

        @pl.when(core == 1)
        def _():
            remote(kvp, kvw.at[7], ks.at[0], kr.at[7], dev_pair).start()

    def kv_pass(k):
        remote(kvp, kvw.at[2 * k], ks.at[k], kr.at[2 * k], line[k]).wait_recv()

        @pl.when(core == 0)
        def _():
            remote(
                kvw.at[2 * k], kvw.at[2 * k + 1], ks.at[3 + k], kr.at[2 * k + 1], dev_pair
            ).start()

        @pl.when(core == 1)
        def _():
            remote(
                kvw.at[2 * k], kvw.at[2 * k - 1], ks.at[3 + k], kr.at[2 * k - 1], dev_pair
            ).start()

    def kv_odd(slot):
        remote(kvw.at[slot], kvw.at[slot], ks.at[0], kr.at[slot], dev_pair).wait_recv()

    sent = ([], [])

    def send_w(core_id, view, device, recv, source=None):
        n = len(sent[core_id])
        target = view()
        src = target if source is None else source
        remote(src, target, ws.at[n], wr.at[recv], device).start()
        sent[core_id].append(view)

    def wait_w(src, recv):
        remote(src, src, ws.at[0], wr.at[recv], dev_y).wait_recv()

    def passed(core_id, n):
        src = wbuf.at[zs[PLANES[n]], :, :, core_id]
        return remote(src, src, pps.at[n], ppr.at[n], dev_pair)

    def pass_plane(core_id, n):
        passed(core_id, n).start()

    low = lax.rem(lax.div(x, 2) * 2, NX)
    high = lax.rem(low + 2, NX)
    mate = low + 1 - lax.rem(x, 2)
    across = 1 - yh

    def sub0(dz, sub):
        row = yh if sub < 2 else across
        return wbuf.at[zs[dz], row, pl.ds(low if sub % 2 == 0 else high, 2), 0]

    def zrecv0(way, hop, sub):
        return 6 + (way * 4 + hop - 1) * 4 + sub

    def away(way, hop):
        return (8 - hop) % 8 if way == 0 else hop

    def near(k):
        row = yh if k < NX else across
        return wbuf.at[z, row, xs[k % NX], 0]

    def ticks0():
        def start(*steps):
            for k in steps:
                device = line[k] if k < NX else (place(z, across, xs[k % NX]), hd)
                send_w(0, lambda: near(0), device, 38 + k, w_hbm)

        def start_z():
            for way in range(2):
                send_w(0, lambda: near(0), dev_z[way], zrecv0(way, 1, 0), w_hbm)

        def shard_at(row, col):
            return wbuf.at[z, row, col, 0]

        def arrive(k):
            row = yh if k < NX else across
            wait_w(wbuf.at[z, row, xs[(NX - k % NX) % NX], 0], 38 + k)

        def all_near():
            for k in range(2, 8):
                if k != 3:
                    arrive(k)
            for sub in range(1, 4):
                zhop(sub, 0)

        def mate_first():
            get_w.wait()
            for k in (1, 3):
                arrive(k)
            for way in range(2):
                send_w(0, lambda: shard_at(yh, mate), dev_z[way], zrecv0(way, 1, 0))

        def zhop(sub, hop):
            for way in range(2):
                half = sub < 2 if way == 0 else sub >= 2
                if hop > 0:
                    if hop == 4 and not half:
                        continue
                    wait_w(sub0(away(way, hop), sub), zrecv0(way, hop, sub))
                if hop < 3 or (hop == 3 and half):
                    send_w(0, lambda way=way: sub0(away(way, hop), sub), dev_z[way],
                           zrecv0(way, hop + 1, sub))

        def give(*planes):
            for n in planes:
                pass_plane(0, n)

        plan = [
            [(start_z,), (start, 1, 3)],
            [(mate_first,)],
            [(all_near,)],
            [(zhop, 0, 1)],
            [(zhop, 1, 1), (zhop, 2, 1), (give, 0)],
            [(zhop, 3, 1), (zhop, 0, 2)],
            [(zhop, 1, 2), (give, 1, 2)],
            [(zhop, 2, 2)],
            [(zhop, 3, 2)],
            [(zhop, 0, 3), (zhop, 1, 3), (give, 3, 4)],
            [(zhop, 2, 3)],
            [(zhop, 3, 3)],
            [(give, 5, 6), (zhop, 0, 4), (zhop, 1, 4)],
            [],
            [(zhop, 2, 4), (zhop, 3, 4), (give, 7)],
            [], [], [],
            [(start, 4, 2, 5, 7, 6)],
        ]
        return [functools.partial(run, steps) for steps in plan]

    def run(steps):
        for step, *values in steps:
            step(*values)

    def ticks1():
        def shard(n, other):
            return wbuf.at[zs[PLANES[n]], across if other else yh, x, 1]

        def beside(n, other, dx):
            return wbuf.at[zs[PLANES[n]], across if other else yh, xs[dx], 1]

        def xrecv(n, other, way):
            return 16 + n * 6 + other * 3 + way

        def yout(*planes):
            for n in planes:
                local = {"source": w_hbm} if n == 0 else {}
                send_w(1, lambda n=n: shard(n, 0), dev_y, 8 + n, **local)

        def xout(*planes):
            for n in planes:
                local = {"source": w_hbm} if n == 0 else {}
                for way in range(2):
                    send_w(1, lambda n=n: shard(n, 0), dev_x[way], xrecv(n, 0, way), **local)

        def turn(*planes):
            for n in planes:
                wait_w(shard(n, 1), 8 + n)
                for way in range(2):
                    send_w(1, lambda n=n: shard(n, 1), dev_x[way], xrecv(n, 1, way))

        def onward(other, *planes):
            for n in planes:
                for way, dx in enumerate((3, 1)):
                    wait_w(beside(n, other, dx), xrecv(n, other, way))
                dx = 1 if other else 3
                send_w(1, lambda n=n: beside(n, other, dx), dev_x[other], xrecv(n, other, 2))

        def give(*planes):
            for n in planes:
                for other in range(2):
                    wait_w(beside(n, other, 2), xrecv(n, other, 2))
                pass_plane(1, n)

        def half(dz, way):
            return wbuf.at[zs[dz], yh, x, 1, pl.ds(16 * way, 16)]

        def zhop(hop):
            for way in range(2):
                dz = away(way, hop)
                if hop == 4:
                    wait_w(half(4, way), way * 4 + 3)
                    continue
                if hop > 0:
                    wait_w(wbuf.at[zs[dz], yh, x, 1], way * 4 + hop - 1)

                def view(dz=dz, way=way):
                    return half(dz, way) if hop == 3 else wbuf.at[zs[dz], yh, x, 1]

                local = {"source": w_hbm} if hop == 0 else {}
                send_w(1, view, dev_z[way], way * 4 + hop, **local)

        plan = [
            [(zhop, 0), (yout, 0)],
            [(zhop, 1), (yout, 1, 2)],
            [(zhop, 2), (yout, 3, 4), (xout, 0, 1, 2)],
            [(zhop, 3), (yout, 5, 6), (turn, 0, 1, 2), (xout, 3, 4)],
            [(zhop, 4), (yout, 7), (onward, 0, 0, 1, 2), (turn, 3, 4), (xout, 5, 6), (onward, 1, 0, 1, 2)],
            [(onward, 0, 3, 4), (turn, 5, 6), (xout, 7), (get_w.wait,), (give, 0)],
            [(onward, 1, 3, 4), (turn, 7), (give, 1, 2)],
            [(onward, 0, 5, 6)],
            [(onward, 1, 5, 6)],
            [(onward, 0, 7), (give, 3, 4)],
            [(onward, 1, 7)],
            [],
            [(give, 5, 6)],
            [],
            [(give, 7)],
            [], [], [], [],
        ]
        return [functools.partial(run, steps) for steps in plan]

    zero_ticks, one_ticks = ticks0(), ticks1()
    assert len(zero_ticks) == len(one_ticks) == 19

    def tick(n):
        pl.when(core == 0)(zero_ticks[n])
        pl.when(core == 1)(one_ticks[n])

    tick(0)
    kv_start()
    tick(18)
    kv_line()

    get_lay.wait()
    first = ctx * 128
    starts, ends, sizes = lay[0:1, :], lay[1:2, :], lay[2:3, :]
    query = first + lax.broadcasted_iota(jnp.int32, (1, 128), 1)
    base = query & (-sizes)
    row = first + lax.broadcasted_iota(jnp.int32, (128, 128), 0)
    inside = (row >= starts) & (row < ends)
    bias[0, 0:128, :] = jnp.where(inside & (row < base), 0.0, NEG)
    bias[1, 0:128, :] = jnp.where(inside & (row < base + sizes), 0.0, NEG)
    bnoisy[...] = jnp.where(inside & (row >= base) & (row < base + sizes), 0.0, NEG)
    for slot in range(1, 8):
        far = jnp.where(row - slot * 128 >= starts, 0.0, NEG)
        bias[0, slot * 128:(slot + 1) * 128, :] = far
        bias[1, slot * 128:(slot + 1) * 128, :] = far

    pltpu.make_async_copy(qs, qs, dsem.at[4]).wait()
    get_kv.wait()
    get_kn.wait()

    def lanes(group):
        return pl.ds(pl.multiple_of(group * 128, 128), 128)

    def keys_of(pair, kind, group):
        return kvw[2 * pair:2 * pair + 2, kind, :, lanes(group)].reshape(256, 128)

    @pl.loop(0, 4)
    def _(i):
        group = lax.div(i, 2)
        pb = group * 4 + lax.rem(i, 2)
        raw = nt(kvn[0, :, lanes(group)], qs[pb])
        masked = bnoisy[...]
        st[pb, 1024:1152, :] = raw + jnp.concatenate([masked, masked], 1)

    def score(pair):
        @pl.loop(0, 8, unroll=4)
        def _(pb):
            group = lax.div(pb, 4)
            raw = nt(keys_of(pair, 0, group), qs[pb])
            masked = bias[lax.div(lax.rem(pb, 4), 2), pair * 256:(pair + 1) * 256, :]
            st[pb, pair * 256:(pair + 1) * 256, :] = raw + jnp.concatenate([masked, masked], 1)

    tick(1)
    kv_before()
    tick(2)
    tick(3)
    kv_pass(1)
    kv_odd(1)
    score(0)
    kv_pass(2)
    kv_odd(3)
    score(1)
    kv_pass(3)
    tick(4)
    kv_odd(5)
    score(2)
    kv_odd(7)
    score(3)
    tick(5)

    def turned(value):
        return value.astype(F32).T.astype(BF16)

    for group in range(2):
        for slot in range(9):
            part = slice(slot * 128, (slot + 1) * 128)
            width = slice(group * 128, (group + 1) * 128)
            for kind, target in ((0, kt), (1, vt)):
                rows = kvn[kind, :, width] if slot == 8 else kvw[slot, kind, :, width]
                target[group, :, part] = turned(rows)


    def softmax(copy_id, low, high):
        count = 9 if copy_id == 0 else 8

        @pl.loop(low, high, unroll=2)
        def _(i):
            group = lax.div(i, 2)
            pair = lax.rem(i, 2)
            pb = group * 4 + copy_id * 2 + pair
            peak = jnp.max(st[pb, 0:128 * count, :], axis=0, keepdims=True)
            total = jnp.zeros((1, 256), F32)
            for block in range(count):
                part = slice(block * 128, (block + 1) * 128)
                weight = jnp.exp2((st[pb, part, :] - peak) * EXP2)
                total = total + jnp.sum(weight, axis=0, keepdims=True)
                pt[pb, part, :] = weight.astype(BF16)
            inverse = 1.0 / total
            lrow[pb] = jnp.broadcast_to(inverse, (8, 256))
            lcol[pb] = jnp.broadcast_to(inverse, (128, 256)).T
            result = nn(vt[group, :, 0:128 * count], pt[pb, 0:128 * count, :]) * inverse
            for half in range(2):
                head = group * 4 + pair * 2 + half
                block = result[:, half * 128:(half + 1) * 128].T.astype(BF16)
                att[copy_id * 128:(copy_id + 1) * 128, lanes(head)] = block

    softmax(1, 0, 2)
    softmax(1, 2, 4)
    tick(6)
    softmax(0, 0, 2)
    softmax(0, 2, 4)
    get_g.wait()

    def plane(n):
        for i in range(2):
            @pl.when(core == 1 - i)
            def _():
                passed(i, n).wait_recv()

        dz = PLANES[n]
        zz = zs[dz]
        lines = [wbuf[zz, line].reshape(256, 1024) for line in range(2)]
        at = pl.multiple_of(zz * 512, 512)
        where = lax.rem(zz, 4)

        @pl.when(lax.div(zz, 4) != hd)
        def _():
            for line in range(2):
                value = nt(att[...], wbuf[zz, line].reshape(256, 1024))
                ysend[where, :, line * 256:(line + 1) * 256] = value.astype(BF16)
            remote(ysend.at[where], yrecv.at[where], es.at[where], er.at[where], dev_head).start()

        rows = gbuf[:, :, pl.ds(at, 512)].reshape(256, 512)
        for piece in range(4):
            part = slice(piece * 256, (piece + 1) * 256)
            term = nn(rows[:, 0:256], lines[0][:, part]) + nn(rows[:, 256:512], lines[1][:, part])
            if n == 0:
                gacc[:, part] = term
            else:
                gacc[:, part] += term

    for n in range(8):
        tick(7 + n)
        plane(n)

    @pl.loop(0, 8, unroll=2)
    def _(pb):
        group = lax.div(pb, 4)
        copy_id = lax.div(lax.rem(pb, 4), 2)
        pair = lax.rem(pb, 2)
        rows = pl.ds(pl.multiple_of(copy_id * 128, 128), 128)
        for half in range(2):
            part = slice(half * 128, (half + 1) * 128)
            head = group * 4 + pair * 2 + half
            grad = gacc[rows, lanes(head)].astype(BF16).astype(F32)
            product = grad * att[rows, lanes(head)].astype(F32)
            delta = jnp.sum(product.T, axis=0, keepdims=True)
            dl[pb, :, part] = jnp.broadcast_to(delta, (8, 128)) * lrow[pb, :, part]
            gs[pb, part, :] = (grad * lcol[pb, part, :]).astype(BF16)

    def grads(keys, values, where, size, group, blocks):
        dk = jnp.zeros((size, 128), F32)
        dv = jnp.zeros((size, 128), F32)
        for b in blocks:
            pb = group * 4 + b
            flow = nt(values, gs[pb])
            weight = pt[pb, where:where + size, :]
            dscore = (weight.astype(F32) * (flow - dl[pb, 0:1, :])).astype(BF16)
            dst[pb, where:where + size, :] = dscore
            dv = dv + nn(weight, gs[pb])
            dk = dk + nn(dscore, qs[pb])
        return dk * SCALE, dv

    def send_odd(pair):
        src = stage.at[pair]

        @pl.when(core == 0)
        def _():
            if pair == 3:
                remote(src, ret.at[3], rs.at[3 + pair], rr.at[3], dev_pair).start()
            else:
                remote(src, col.at[pair], rs.at[3 + pair], rr.at[4 + pair], dev_pair).start()

        @pl.when(core == 1)
        def _():
            if pair == 0:
                remote(src, ret.at[3], rs.at[3 + pair], rr.at[3], dev_pair).start()
            else:
                remote(src, col.at[pair - 1], rs.at[3 + pair], rr.at[3 + pair], dev_pair).start()

    def collect(k):
        remote(col.at[k - 1], col.at[k - 1], rs.at[0], rr.at[3 + k], dev_pair).wait_recv()
        comb[k - 1] = (evens[k - 1] + col[k - 1].astype(F32)).astype(BF16)
        remote(comb.at[k - 1], ret.at[k - 1], rs.at[k - 1], rr.at[k - 1], line[NX - k]).start()

    for pair in (3, 2, 1, 0):
        @pl.loop(0, 2, unroll=2)
        def _(group):
            dk, dv = grads(
                keys_of(pair, 0, group), keys_of(pair, 1, group), pair * 256, 256, group, range(4)
            )
            for kind, value in ((0, dk), (1, dv)):
                if pair == 0:
                    own[kind, :, lanes(group)] = value[0:128]
                else:
                    evens[pair - 1, kind, :, lanes(group)] = value[0:128]
                stage[pair, kind, :, lanes(group)] = value[128:256].astype(BF16)

        send_odd(pair)
        if pair < 3:
            @pl.when(core == 0)
            def _():
                collect(pair + 1)
        if pair < 2:
            @pl.when(core == 1)
            def _():
                collect(pair + 2)

    @pl.loop(0, 2)
    def _(group):
        dk, dv = grads(
            kvn[0, :, lanes(group)], kvn[1, :, lanes(group)], 1024, 128, group, range(2)
        )
        dkvv[0, 0, :, lanes(group)] = dk
        dkvv[1, 0, :, lanes(group)] = dv

    def dqueries(copy_id):
        count = 1152 if copy_id == 0 else 1024

        @pl.loop(0, 4, unroll=2)
        def _(i):
            group = lax.div(i, 2)
            pair = lax.rem(i, 2)
            pb = group * 4 + copy_id * 2 + pair
            result = nn(kt[group, :, 0:count], dst[pb, 0:count, :]) * SCALE
            for half in range(2):
                head = group * 4 + pair * 2 + half
                dqv[copy_id, :, lanes(head)] = result[:, half * 128:(half + 1) * 128].T


    pl.when(core == 1)(functools.partial(collect, 1))
    dqueries(0)

    def line_sums():
        for n in (2, 1, 0, 3):
            remote(ret.at[n], ret.at[n], rs.at[n], rr.at[n], dev_pair).wait_recv()
        for kind in range(2):
            mine, other = own[kind], jnp.zeros((128, 256), F32)
            for n in range(4):
                here = core == 0 if n == 3 else x + n + 1 < NX
                value = ret[n, kind].astype(F32)
                mine = mine + jnp.where(here, value, 0.0)
                other = other + jnp.where(here, 0.0, value)
            own[kind] = mine
            back[kind] = other.astype(BF16)
        remote(back, retp, rs.at[7], rr.at[7], dev_before).start()

    line_sums()
    dqueries(1)

    def mine(j):
        for line_id in range(2):
            part = slice(line_id * 256, (line_id + 1) * 256)
            ypart[j, :, part] = nt(att[...], wbuf[hd * 4 + j, line_id].reshape(256, 1024))

    for j in range(4):
        mine(j)

    def finish(j):
        remote(ysend.at[j], yrecv.at[j], es.at[j], er.at[j], dev_head).wait_recv()
        part = slice(j * 512, (j + 1) * 512)
        total = ypart[j] + yrecv[j].astype(F32)
        for copy_id in range(2):
            yout[copy_id, :, part] = total[copy_id * 128:(copy_id + 1) * 128].astype(BF16)

    for j in range(4):
        finish(j)

    def last_sum():
        remote(back, retp, rs.at[7], rr.at[7], dev_before).wait_recv()
        for kind in range(2):
            dkvv[kind, 1] = own[kind] + retp[kind].astype(F32)

    last_sum()

    for n in range(8):
        remote(own_kv, kvp, ks.at[n], kr.at[0], dev_after).wait_send()
    for i in range(2):
        @pl.when(core == i)
        def _():
            for n, view in enumerate(sent[i]):
                remote(view(), view(), ws.at[n], wr.at[0], dev_y).wait_send()
            for n in range(8):
                passed(i, n).wait_send()

    for j in range(4):
        remote(ysend.at[j], yrecv.at[j], es.at[j], er.at[j], dev_head).wait_send()
    for n in range(8):
        remote(stage.at[0], stage.at[0], rs.at[n], rr.at[0], dev_pair).wait_send()


def per_device(queries, keys_values, grad_layer, out_proj, doc_layout):
    vm = pltpu.VMEM
    dma = pltpu.SemaphoreType.DMA
    scratch = [
        vm((NZ, NY, NX, 2, 32, 1024), BF16),
        vm((8, 256, 128), BF16),
        vm((8, 2, 128, 256), BF16),
        vm((2, 128, 256), BF16),
        vm((2, 128, 256), BF16),
        vm((2, 128, 4096), BF16),
        vm((3, 128), jnp.int32),
        vm((2, 1024, 128), F32),
        vm((128, 128), F32),
        vm((8, 1152, 256), F32),
        vm((8, 1152, 256), BF16),
        vm((8, 1152, 256), BF16),
        vm((2, 128, 1152), BF16),
        vm((2, 128, 1152), BF16),
        vm((256, 1024), BF16),
        vm((256, 1024), F32),
        vm((8, 8, 256), F32),
        vm((8, 256, 128), F32),
        vm((8, 256, 128), BF16),
        vm((8, 8, 256), F32),
        vm((4, 256, 512), F32),
        vm((4, 256, 512), BF16),
        vm((4, 256, 512), BF16),
        vm((4, 2, 128, 256), BF16),
        vm((3, 2, 128, 256), F32),
        vm((3, 2, 128, 256), BF16),
        vm((3, 2, 128, 256), BF16),
        vm((4, 2, 128, 256), BF16),
        vm((2, 128, 256), BF16),
        vm((2, 128, 256), BF16),
        vm((2, 128, 256), F32),
        dma((8,)), dma((8,)), dma((8,)), dma((72,)), dma((72,)),
        dma((8,)), dma((8,)), dma((4,)), dma((4,)), dma((8,)), dma((8,)),
    ]
    anywhere = pl.BlockSpec(memory_space=pl.ANY)
    near = pl.BlockSpec(memory_space=pltpu.VMEM)
    shapes = (((2, 128, 2048), BF16), ((2, 128, 1024), F32), ((2, 2, 128, 256), F32))
    results = pl.pallas_call(
        kernel,
        out_shape=tuple(pltpu.VMEM(*shape) for shape in shapes),
        in_specs=[anywhere] * 5,
        out_specs=(near,) * 3,
        scratch_shapes=scratch,
        compiler_params=pltpu.CompilerParams(
            collective_id=0, has_side_effects=True, vmem_limit_bytes=56 * 1024 * 1024
        ),
    )(queries, keys_values, grad_layer, out_proj, doc_layout)
    return pl.pallas_call(
        put_out,
        out_shape=tuple(jax.ShapeDtypeStruct(*shape) for shape in shapes),
        in_specs=[near] * 3,
        out_specs=(anywhere,) * 3,
        scratch_shapes=[dma((3,))],
        compiler_params=pltpu.CompilerParams(vmem_limit_bytes=4 * 1024 * 1024),
    )(*results)


def put_out(a, b, c, out_a, out_b, out_c, sem):
    copies = [
        pltpu.make_async_copy(src, target, sem.at[n])
        for n, (src, target) in enumerate(((a, out_a), (b, out_b), (c, out_c)))
    ]
    for copy in copies:
        copy.start()
    for copy in copies:
        copy.wait()


def solution(mesh):
    return jax.shard_map(
        per_device,
        mesh=mesh,
        in_specs=(
            P(None, "ctx", "head"),
            P(None, None, "ctx", "head"),
            P(None, "ctx", None),
            P("ctx", "head"),
            P(None, "ctx"),
        ),
        out_specs=(P(None, "ctx", "head"), P(None, "ctx", "head"), P(None, None, "ctx", "head")),
        check_vma=False,
    )
```

```python
import functools
import math

import jax
import jax.numpy as jnp
from jax import lax
from jax.experimental import pallas as pl
from jax.experimental.pallas import tpu as pltpu
from jax.sharding import PartitionSpec as P

F32 = jnp.float32
BF16 = jnp.bfloat16
MESH = pl.DeviceIdType.MESH
NEG = -1e30
SCALE = 128 ** -0.5
EXP2 = SCALE * math.log2(math.e)

NZ, NY, NX = 8, 2, 4
SUBS = (0, 3, 1, 2)
PLANES = (0, 7, 1, 6, 2, 5, 3, 4)


def nt(a, b):
    return lax.dot_general(a, b, (((1,), (1,)), ((), ())), preferred_element_type=F32)


def nn(a, b):
    return lax.dot_general(a, b, (((1,), (0,)), ((), ())), preferred_element_type=F32)


def kernel(
    q_hbm, kv_hbm, g_hbm, w_hbm, lay_hbm,
    yout, dqv, dkvv,
    wbuf, qs, kvw, kvp, kvn, gbuf, lay, bias, bnoisy, st, pt, dst, vt, kt,
    att, gacc, lrow, lcol, gs, dl, ypart, ysend, yrecv,
    stage, evens, col, comb, ret, back, retp, own,
    dsem, ks, kr, ws, wr, pps, ppr, es, er, rs, rr,
):
    ctx = lax.axis_index("ctx")
    hd = lax.axis_index("head")
    core = lax.rem(ctx, 2)
    x = lax.rem(lax.div(ctx, 2), NX)
    yh = lax.rem(lax.div(ctx, 8), NY)
    z = lax.div(ctx, 16)

    def place(z_, y_, x_):
        return ((z_ * NY + y_) * NX + x_) * 2 + core

    xs = [lax.rem(x + d, NX) for d in range(NX)]
    zs = [lax.rem(z + d, NZ) for d in range(NZ)]
    dev_y = (place(z, 1 - yh, x), hd)
    dev_x = [(place(z, yh, xs[1]), hd), (place(z, yh, xs[3]), hd)]
    dev_z = [(place(zs[1], yh, x), hd), (place(zs[7], yh, x), hd)]
    dev_pair = (ctx + 1 - 2 * core, hd)
    dev_head = (ctx, 1 - hd)
    line = [(place(z, yh, xs[k]), hd) for k in range(NX)]
    dev_after = (lax.rem(ctx + 8, 128), hd)
    dev_before = (lax.rem(ctx + 120, 128), hd)

    def remote(src, dst_ref, send, recv, device):
        return pltpu.make_async_remote_copy(
            src_ref=src, dst_ref=dst_ref, send_sem=send, recv_sem=recv,
            device_id=device, device_id_type=MESH,
        )

    def fetch(src, dst_ref, sem):
        copy = pltpu.make_async_copy(src, dst_ref, sem)
        copy.start()
        return copy

    get_w = fetch(w_hbm, wbuf.at[z, yh, x, core], dsem.at[0])
    get_kv = fetch(kv_hbm.at[:, 1], kvw.at[0], dsem.at[1])
    get_kn = fetch(kv_hbm.at[:, 0], kvn, dsem.at[2])
    get_lay = fetch(lay_hbm, lay, dsem.at[3])
    for copy_id in range(2):
        for head in range(8):
            pb = (head // 4) * 4 + copy_id * 2 + (head % 4) // 2
            fetch(
                q_hbm.at[copy_id, :, pl.ds(head * 128, 128)],
                qs.at[pb, pl.ds((head % 2) * 128, 128)],
                dsem.at[4],
            )
    get_g = fetch(g_hbm, gbuf, dsem.at[5])

    barrier = pltpu.get_barrier_semaphore()
    planar = [(place(z, 1 - yh, xs[k]), hd) for k in range(NX)]
    meet = [*planar, *line[1:], *dev_z, dev_pair, dev_head, dev_after, dev_before]
    for device in meet:
        pl.semaphore_signal(barrier, inc=1, device_id=device, device_id_type=MESH)
    pl.semaphore_wait(barrier, len(meet))

    own_kv = kv_hbm.at[:, 1]
    kv_next = remote(own_kv, kvp, ks.at[7], kr.at[0], dev_after)

    def kv_start():
        kv_next.start()

        @pl.when(core == 0)
        def _():
            remote(own_kv, kvw.at[1], ks.at[0], kr.at[1], dev_pair).start()

    def kv_line():
        for k in (1, 2, 3):
            @pl.when(x + k < NX)
            def _():
                remote(own_kv, kvw.at[2 * k], ks.at[k], kr.at[2 * k], line[k]).start()

    def kv_before():
        kv_next.wait_recv()
        for k in (1, 2, 3):
            @pl.when(x + k >= NX)
            def _():
                remote(kvp, kvw.at[2 * k], ks.at[k], kr.at[2 * k], line[k]).start()

        @pl.when(core == 1)
        def _():
            remote(kvp, kvw.at[7], ks.at[0], kr.at[7], dev_pair).start()

    def kv_pass(k):
        remote(kvp, kvw.at[2 * k], ks.at[k], kr.at[2 * k], line[k]).wait_recv()

        @pl.when(core == 0)
        def _():
            remote(
                kvw.at[2 * k], kvw.at[2 * k + 1], ks.at[3 + k], kr.at[2 * k + 1], dev_pair
            ).start()

        @pl.when(core == 1)
        def _():
            remote(
                kvw.at[2 * k], kvw.at[2 * k - 1], ks.at[3 + k], kr.at[2 * k - 1], dev_pair
            ).start()

    def kv_odd(slot):
        remote(kvw.at[slot], kvw.at[slot], ks.at[0], kr.at[slot], dev_pair).wait_recv()

    sent = ([], [])

    def send_w(core_id, view, device, recv, source=None):
        n = len(sent[core_id])
        target = view()
        src = target if source is None else source
        remote(src, target, ws.at[n], wr.at[recv], device).start()
        sent[core_id].append(view)

    def wait_w(src, recv):
        remote(src, src, ws.at[0], wr.at[recv], dev_y).wait_recv()

    def passed(core_id, n):
        src = wbuf.at[zs[PLANES[n]], :, :, core_id]
        return remote(src, src, pps.at[n], ppr.at[n], dev_pair)

    def pass_plane(core_id, n):
        passed(core_id, n).start()

    low = lax.rem(lax.div(x, 2) * 2, NX)
    high = lax.rem(low + 2, NX)
    mate = low + 1 - lax.rem(x, 2)
    across = 1 - yh

    def sub0(dz, sub):
        row = yh if sub < 2 else across
        return wbuf.at[zs[dz], row, pl.ds(low if sub % 2 == 0 else high, 2), 0]

    def zrecv0(way, hop, sub):
        return 6 + (way * 4 + hop - 1) * 4 + sub

    def away(way, hop):
        return (8 - hop) % 8 if way == 0 else hop

    def near(k):
        row = yh if k < NX else across
        return wbuf.at[z, row, xs[k % NX], 0]

    def ticks0():
        def start(*steps):
            for k in steps:
                device = line[k] if k < NX else (place(z, across, xs[k % NX]), hd)
                send_w(0, lambda: near(0), device, 38 + k, w_hbm)

        def start_z():
            for way in range(2):
                send_w(0, lambda: near(0), dev_z[way], zrecv0(way, 1, 0), w_hbm)

        def shard_at(row, col):
            return wbuf.at[z, row, col, 0]

        def arrive(k):
            row = yh if k < NX else across
            wait_w(wbuf.at[z, row, xs[(NX - k % NX) % NX], 0], 38 + k)

        def all_near():
            for k in range(2, 8):
                if k != 3:
                    arrive(k)
            for sub in range(1, 4):
                zhop(sub, 0)

        def mate_first():
            get_w.wait()
            for k in (1, 3):
                arrive(k)
            for way in range(2):
                send_w(0, lambda: shard_at(yh, mate), dev_z[way], zrecv0(way, 1, 0))

        def zhop(sub, hop):
            for way in range(2):
                half = sub < 2 if way == 0 else sub >= 2
                if hop > 0:
                    if hop == 4 and not half:
                        continue
                    wait_w(sub0(away(way, hop), sub), zrecv0(way, hop, sub))
                if hop < 3 or (hop == 3 and half):
                    send_w(0, lambda way=way: sub0(away(way, hop), sub), dev_z[way],
                           zrecv0(way, hop + 1, sub))

        def give(*planes):
            for n in planes:
                pass_plane(0, n)

        plan = [
            [(start_z,), (start, 1, 3)],
            [(mate_first,)],
            [(all_near,)],
            [(zhop, 0, 1), (give, 0)],
            [(zhop, 1, 1), (zhop, 2, 1)],
            [(zhop, 3, 1), (give, 1, 2), (zhop, 0, 2)],
            [(zhop, 1, 2)],
            [(zhop, 2, 2)],
            [(zhop, 3, 2), (give, 3, 4)],
            [(zhop, 0, 3), (zhop, 1, 3)],
            [(zhop, 2, 3)],
            [(zhop, 3, 3), (give, 5, 6)],
            [(zhop, 0, 4), (zhop, 1, 4)],
            [(zhop, 2, 4), (zhop, 3, 4), (give, 7)],
            [],
            [], [], [],
            [(start, 4, 2, 5, 7, 6)],
        ]
        return [functools.partial(run, steps) for steps in plan]

    def run(steps):
        for step, *values in steps:
            step(*values)

    def ticks1():
        def shard(n, other):
            return wbuf.at[zs[PLANES[n]], across if other else yh, x, 1]

        def beside(n, other, dx):
            return wbuf.at[zs[PLANES[n]], across if other else yh, xs[dx], 1]

        def xrecv(n, other, way):
            return 16 + n * 6 + other * 3 + way

        def yout(*planes):
            for n in planes:
                local = {"source": w_hbm} if n == 0 else {}
                send_w(1, lambda n=n: shard(n, 0), dev_y, 8 + n, **local)

        def xout(*planes):
            for n in planes:
                local = {"source": w_hbm} if n == 0 else {}
                for way in range(2):
                    send_w(1, lambda n=n: shard(n, 0), dev_x[way], xrecv(n, 0, way), **local)

        def turn(*planes):
            for n in planes:
                wait_w(shard(n, 1), 8 + n)
                for way in range(2):
                    send_w(1, lambda n=n: shard(n, 1), dev_x[way], xrecv(n, 1, way))

        def onward(other, *planes):
            for n in planes:
                for way, dx in enumerate((3, 1)):
                    wait_w(beside(n, other, dx), xrecv(n, other, way))
                dx = 1 if other else 3
                send_w(1, lambda n=n: beside(n, other, dx), dev_x[other], xrecv(n, other, 2))

        def give(*planes):
            for n in planes:
                for other in range(2):
                    wait_w(beside(n, other, 2), xrecv(n, other, 2))
                pass_plane(1, n)

        def half(dz, way):
            return wbuf.at[zs[dz], yh, x, 1, pl.ds(16 * way, 16)]

        def zhop(hop):
            for way in range(2):
                dz = away(way, hop)
                if hop == 4:
                    wait_w(half(4, way), way * 4 + 3)
                    continue
                if hop > 0:
                    wait_w(wbuf.at[zs[dz], yh, x, 1], way * 4 + hop - 1)

                def view(dz=dz, way=way):
                    return half(dz, way) if hop == 3 else wbuf.at[zs[dz], yh, x, 1]

                local = {"source": w_hbm} if hop == 0 else {}
                send_w(1, view, dev_z[way], way * 4 + hop, **local)

        plan = [
            [(zhop, 0), (yout, 0)],
            [(zhop, 1), (yout, 1, 2)],
            [(zhop, 2), (yout, 3, 4), (xout, 0, 1, 2)],
            [(zhop, 3), (yout, 5, 6), (turn, 0, 1, 2), (xout, 3, 4)],
            [(zhop, 4), (yout, 7), (onward, 0, 0, 1, 2), (turn, 3, 4), (xout, 5, 6), (onward, 1, 0, 1, 2)],
            [(onward, 0, 3, 4), (turn, 5, 6), (xout, 7), (get_w.wait,), (give, 0)],
            [(onward, 1, 3, 4), (turn, 7), (give, 1, 2)],
            [(onward, 0, 5, 6)],
            [(onward, 1, 5, 6)],
            [(onward, 0, 7), (give, 3, 4)],
            [(onward, 1, 7)],
            [(give, 5, 6)],
            [],
            [(give, 7)],
            [],
            [], [], [], [],
        ]
        return [functools.partial(run, steps) for steps in plan]

    zero_ticks, one_ticks = ticks0(), ticks1()
    assert len(zero_ticks) == len(one_ticks) == 19

    def tick(n):
        pl.when(core == 0)(zero_ticks[n])
        pl.when(core == 1)(one_ticks[n])

    tick(0)
    kv_start()
    tick(18)
    kv_line()

    get_lay.wait()
    first = ctx * 128
    starts, ends, sizes = lay[0:1, :], lay[1:2, :], lay[2:3, :]
    query = first + lax.broadcasted_iota(jnp.int32, (1, 128), 1)
    base = query & (-sizes)
    row = first + lax.broadcasted_iota(jnp.int32, (128, 128), 0)
    inside = (row >= starts) & (row < ends)
    bias[0, 0:128, :] = jnp.where(inside & (row < base), 0.0, NEG)
    bias[1, 0:128, :] = jnp.where(inside & (row < base + sizes), 0.0, NEG)
    bnoisy[...] = jnp.where(inside & (row >= base) & (row < base + sizes), 0.0, NEG)
    for slot in range(1, 8):
        far = jnp.where(row - slot * 128 >= starts, 0.0, NEG)
        bias[0, slot * 128:(slot + 1) * 128, :] = far
        bias[1, slot * 128:(slot + 1) * 128, :] = far

    pltpu.make_async_copy(qs, qs, dsem.at[4]).wait()
    get_kv.wait()
    get_kn.wait()

    def lanes(group):
        return pl.ds(pl.multiple_of(group * 128, 128), 128)

    def keys_of(pair, kind, group):
        return kvw[2 * pair:2 * pair + 2, kind, :, lanes(group)].reshape(256, 128)

    @pl.loop(0, 4)
    def _(i):
        group = lax.div(i, 2)
        pb = group * 4 + lax.rem(i, 2)
        raw = nt(kvn[0, :, lanes(group)], qs[pb])
        masked = bnoisy[...]
        st[pb, 1024:1152, :] = raw + jnp.concatenate([masked, masked], 1)

    def score(pair):
        @pl.loop(0, 8, unroll=4)
        def _(pb):
            group = lax.div(pb, 4)
            raw = nt(keys_of(pair, 0, group), qs[pb])
            masked = bias[lax.div(lax.rem(pb, 4), 2), pair * 256:(pair + 1) * 256, :]
            st[pb, pair * 256:(pair + 1) * 256, :] = raw + jnp.concatenate([masked, masked], 1)

    tick(1)
    kv_before()
    tick(2)
    tick(3)
    kv_pass(1)
    kv_odd(1)
    score(0)
    kv_pass(2)
    kv_odd(3)
    score(1)
    kv_pass(3)
    tick(4)
    kv_odd(5)
    score(2)
    kv_odd(7)
    score(3)
    tick(5)

    def turned(value):
        return value.astype(F32).T.astype(BF16)

    for group in range(2):
        for slot in range(9):
            part = slice(slot * 128, (slot + 1) * 128)
            width = slice(group * 128, (group + 1) * 128)
            for kind, target in ((0, kt), (1, vt)):
                rows = kvn[kind, :, width] if slot == 8 else kvw[slot, kind, :, width]
                target[group, :, part] = turned(rows)


    def softmax(copy_id, low, high):
        count = 9 if copy_id == 0 else 8

        @pl.loop(low, high, unroll=2)
        def _(i):
            group = lax.div(i, 2)
            pair = lax.rem(i, 2)
            pb = group * 4 + copy_id * 2 + pair
            peak = jnp.max(st[pb, 0:128 * count, :], axis=0, keepdims=True)
            total = jnp.zeros((1, 256), F32)
            for block in range(count):
                part = slice(block * 128, (block + 1) * 128)
                weight = jnp.exp2((st[pb, part, :] - peak) * EXP2)
                total = total + jnp.sum(weight, axis=0, keepdims=True)
                pt[pb, part, :] = weight.astype(BF16)
            inverse = 1.0 / total
            lrow[pb] = jnp.broadcast_to(inverse, (8, 256))
            lcol[pb] = jnp.broadcast_to(inverse, (128, 256)).T
            result = nn(vt[group, :, 0:128 * count], pt[pb, 0:128 * count, :]) * inverse
            for half in range(2):
                head = group * 4 + pair * 2 + half
                block = result[:, half * 128:(half + 1) * 128].T.astype(BF16)
                att[copy_id * 128:(copy_id + 1) * 128, lanes(head)] = block

    softmax(1, 0, 2)
    softmax(1, 2, 4)
    tick(6)
    softmax(0, 0, 2)
    softmax(0, 2, 4)
    get_g.wait()

    def plane(n):
        for i in range(2):
            @pl.when(core == 1 - i)
            def _():
                passed(i, n).wait_recv()

        dz = PLANES[n]
        zz = zs[dz]
        lines = [wbuf[zz, line].reshape(256, 1024) for line in range(2)]
        at = pl.multiple_of(zz * 512, 512)
        where = lax.rem(zz, 4)

        @pl.when(lax.div(zz, 4) != hd)
        def _():
            for line in range(2):
                value = nt(att[...], wbuf[zz, line].reshape(256, 1024))
                ysend[where, :, line * 256:(line + 1) * 256] = value.astype(BF16)
            remote(ysend.at[where], yrecv.at[where], es.at[where], er.at[where], dev_head).start()

        rows = gbuf[:, :, pl.ds(at, 512)].reshape(256, 512)
        for piece in range(4):
            part = slice(piece * 256, (piece + 1) * 256)
            term = nn(rows[:, 0:256], lines[0][:, part]) + nn(rows[:, 256:512], lines[1][:, part])
            if n == 0:
                gacc[:, part] = term
            else:
                gacc[:, part] += term

    for n in range(8):
        tick(7 + n)
        plane(n)

    @pl.loop(0, 8, unroll=2)
    def _(pb):
        group = lax.div(pb, 4)
        copy_id = lax.div(lax.rem(pb, 4), 2)
        pair = lax.rem(pb, 2)
        rows = pl.ds(pl.multiple_of(copy_id * 128, 128), 128)
        for half in range(2):
            part = slice(half * 128, (half + 1) * 128)
            head = group * 4 + pair * 2 + half
            grad = gacc[rows, lanes(head)].astype(BF16).astype(F32)
            product = grad * att[rows, lanes(head)].astype(F32)
            delta = jnp.sum(product.T, axis=0, keepdims=True)
            dl[pb, :, part] = jnp.broadcast_to(delta, (8, 128)) * lrow[pb, :, part]
            gs[pb, part, :] = (grad * lcol[pb, part, :]).astype(BF16)

    def grads(keys, values, where, size, group, blocks):
        dk = jnp.zeros((size, 128), F32)
        dv = jnp.zeros((size, 128), F32)
        for b in blocks:
            pb = group * 4 + b
            flow = nt(values, gs[pb])
            weight = pt[pb, where:where + size, :]
            dscore = (weight.astype(F32) * (flow - dl[pb, 0:1, :])).astype(BF16)
            dst[pb, where:where + size, :] = dscore
            dv = dv + nn(weight, gs[pb])
            dk = dk + nn(dscore, qs[pb])
        return dk * SCALE, dv

    def send_odd(pair):
        src = stage.at[pair]

        @pl.when(core == 0)
        def _():
            if pair == 3:
                remote(src, ret.at[3], rs.at[3 + pair], rr.at[3], dev_pair).start()
            else:
                remote(src, col.at[pair], rs.at[3 + pair], rr.at[4 + pair], dev_pair).start()

        @pl.when(core == 1)
        def _():
            if pair == 0:
                remote(src, ret.at[3], rs.at[3 + pair], rr.at[3], dev_pair).start()
            else:
                remote(src, col.at[pair - 1], rs.at[3 + pair], rr.at[3 + pair], dev_pair).start()

    def collect(k):
        remote(col.at[k - 1], col.at[k - 1], rs.at[0], rr.at[3 + k], dev_pair).wait_recv()
        comb[k - 1] = (evens[k - 1] + col[k - 1].astype(F32)).astype(BF16)
        remote(comb.at[k - 1], ret.at[k - 1], rs.at[k - 1], rr.at[k - 1], line[NX - k]).start()

    for pair in (3, 2, 1, 0):
        @pl.loop(0, 2, unroll=2)
        def _(group):
            dk, dv = grads(
                keys_of(pair, 0, group), keys_of(pair, 1, group), pair * 256, 256, group, range(4)
            )
            for kind, value in ((0, dk), (1, dv)):
                if pair == 0:
                    own[kind, :, lanes(group)] = value[0:128]
                else:
                    evens[pair - 1, kind, :, lanes(group)] = value[0:128]
                stage[pair, kind, :, lanes(group)] = value[128:256].astype(BF16)

        send_odd(pair)
        if pair < 3:
            @pl.when(core == 0)
            def _():
                collect(pair + 1)
        if pair < 2:
            @pl.when(core == 1)
            def _():
                collect(pair + 2)

    pl.when(core == 1)(functools.partial(collect, 1))

    @pl.loop(0, 2)
    def _(group):
        dk, dv = grads(
            kvn[0, :, lanes(group)], kvn[1, :, lanes(group)], 1024, 128, group, range(2)
        )
        dkvv[0, 0, :, lanes(group)] = dk
        dkvv[1, 0, :, lanes(group)] = dv

    def dqueries(copy_id):
        count = 1152 if copy_id == 0 else 1024

        @pl.loop(0, 4, unroll=2)
        def _(i):
            group = lax.div(i, 2)
            pair = lax.rem(i, 2)
            pb = group * 4 + copy_id * 2 + pair
            result = nn(kt[group, :, 0:count], dst[pb, 0:count, :]) * SCALE
            for half in range(2):
                head = group * 4 + pair * 2 + half
                dqv[copy_id, :, lanes(head)] = result[:, half * 128:(half + 1) * 128].T


    dqueries(0)
    dqueries(1)

    def line_sums():
        for n in (2, 1, 0, 3):
            remote(ret.at[n], ret.at[n], rs.at[n], rr.at[n], dev_pair).wait_recv()
        for kind in range(2):
            mine, other = own[kind], jnp.zeros((128, 256), F32)
            for n in range(4):
                here = core == 0 if n == 3 else x + n + 1 < NX
                value = ret[n, kind].astype(F32)
                mine = mine + jnp.where(here, value, 0.0)
                other = other + jnp.where(here, 0.0, value)
            own[kind] = mine
            back[kind] = other.astype(BF16)
        remote(back, retp, rs.at[7], rr.at[7], dev_before).start()

    def mine(j):
        for line_id in range(2):
            part = slice(line_id * 256, (line_id + 1) * 256)
            ypart[j, :, part] = nt(att[...], wbuf[hd * 4 + j, line_id].reshape(256, 1024))

    for j in range(4):
        mine(j)
    line_sums()

    def finish(j):
        remote(ysend.at[j], yrecv.at[j], es.at[j], er.at[j], dev_head).wait_recv()
        part = slice(j * 512, (j + 1) * 512)
        total = ypart[j] + yrecv[j].astype(F32)
        for copy_id in range(2):
            yout[copy_id, :, part] = total[copy_id * 128:(copy_id + 1) * 128].astype(BF16)

    for j in range(4):
        finish(j)

    def last_sum():
        remote(back, retp, rs.at[7], rr.at[7], dev_before).wait_recv()
        for kind in range(2):
            dkvv[kind, 1] = own[kind] + retp[kind].astype(F32)

    last_sum()

    for n in range(8):
        remote(own_kv, kvp, ks.at[n], kr.at[0], dev_after).wait_send()
    for i in range(2):
        @pl.when(core == i)
        def _():
            for n, view in enumerate(sent[i]):
                remote(view(), view(), ws.at[n], wr.at[0], dev_y).wait_send()
            for n in range(8):
                passed(i, n).wait_send()

    for j in range(4):
        remote(ysend.at[j], yrecv.at[j], es.at[j], er.at[j], dev_head).wait_send()
    for n in range(8):
        remote(stage.at[0], stage.at[0], rs.at[n], rr.at[0], dev_pair).wait_send()


def per_device(queries, keys_values, grad_layer, out_proj, doc_layout):
    vm = pltpu.VMEM
    dma = pltpu.SemaphoreType.DMA
    scratch = [
        vm((NZ, NY, NX, 2, 32, 1024), BF16),
        vm((8, 256, 128), BF16),
        vm((8, 2, 128, 256), BF16),
        vm((2, 128, 256), BF16),
        vm((2, 128, 256), BF16),
        vm((2, 128, 4096), BF16),
        vm((3, 128), jnp.int32),
        vm((2, 1024, 128), F32),
        vm((128, 128), F32),
        vm((8, 1152, 256), F32),
        vm((8, 1152, 256), BF16),
        vm((8, 1152, 256), BF16),
        vm((2, 128, 1152), BF16),
        vm((2, 128, 1152), BF16),
        vm((256, 1024), BF16),
        vm((256, 1024), F32),
        vm((8, 8, 256), F32),
        vm((8, 256, 128), F32),
        vm((8, 256, 128), BF16),
        vm((8, 8, 256), F32),
        vm((4, 256, 512), F32),
        vm((4, 256, 512), BF16),
        vm((4, 256, 512), BF16),
        vm((4, 2, 128, 256), BF16),
        vm((3, 2, 128, 256), F32),
        vm((3, 2, 128, 256), BF16),
        vm((3, 2, 128, 256), BF16),
        vm((4, 2, 128, 256), BF16),
        vm((2, 128, 256), BF16),
        vm((2, 128, 256), BF16),
        vm((2, 128, 256), F32),
        dma((8,)), dma((8,)), dma((8,)), dma((72,)), dma((72,)),
        dma((8,)), dma((8,)), dma((4,)), dma((4,)), dma((8,)), dma((8,)),
    ]
    anywhere = pl.BlockSpec(memory_space=pl.ANY)
    near = pl.BlockSpec(memory_space=pltpu.VMEM)
    shapes = (((2, 128, 2048), BF16), ((2, 128, 1024), F32), ((2, 2, 128, 256), F32))
    results = pl.pallas_call(
        kernel,
        out_shape=tuple(pltpu.VMEM(*shape) for shape in shapes),
        in_specs=[anywhere] * 5,
        out_specs=(near,) * 3,
        scratch_shapes=scratch,
        compiler_params=pltpu.CompilerParams(
            collective_id=0, has_side_effects=True, vmem_limit_bytes=56 * 1024 * 1024
        ),
    )(queries, keys_values, grad_layer, out_proj, doc_layout)
    return pl.pallas_call(
        put_out,
        out_shape=tuple(jax.ShapeDtypeStruct(*shape) for shape in shapes),
        in_specs=[near] * 3,
        out_specs=(anywhere,) * 3,
        scratch_shapes=[dma((3,))],
        compiler_params=pltpu.CompilerParams(vmem_limit_bytes=4 * 1024 * 1024),
    )(*results)


def put_out(a, b, c, out_a, out_b, out_c, sem):
    copies = [
        pltpu.make_async_copy(src, target, sem.at[n])
        for n, (src, target) in enumerate(((a, out_a), (b, out_b), (c, out_c)))
    ]
    for copy in copies:
        copy.start()
    for copy in copies:
        copy.wait()


def solution(mesh):
    return jax.shard_map(
        per_device,
        mesh=mesh,
        in_specs=(
            P(None, "ctx", "head"),
            P(None, None, "ctx", "head"),
            P(None, "ctx", None),
            P("ctx", "head"),
            P(None, "ctx"),
        ),
        out_specs=(P(None, "ctx", "head"), P(None, "ctx", "head"), P(None, None, "ctx", "head")),
        check_vma=False,
    )
```
